32 devices in a mesh: ctx: 8 (over z, x), head: 4 (over y, core).
Axes of the slice: x: 2, y: 2, z: 4, core: 2. Of those that a mesh axis runs over, the one named last changes fastest.
Arguments:
- tokens: bfloat16 [2048, 4096], P('ctx', 'head'), may hold values from -96 to 96
- w_query: bfloat16 [4096, 2048], P(None, 'head'), may hold values from -0.1875 to 0.1875
- key_matrix: bfloat16 [4096, 512], P(None, 'head'), may hold values from -0.09375 to 0.09375
- value_matrix: bfloat16 [4096, 512], P(None, 'head'), may hold values from -0.09375 to 0.09375
- w_output: bfloat16 [2048, 4096], P('head'), may hold values from -0.125 to 0.125
Outputs:
- mixed: bfloat16 [2048, 4096], P('ctx', 'head')
The draws below stay inside these ranges and needn't reach their ends.
All inputs are finite; a program needn't handle non-finite values.
Results may differ from the reference program's by a relative error of at most 0.013.
The reference program's roundings to bfloat16 on the way (of `query`, `keys`, `values`, `rounded` and `attended`) count: a program that leaves them out, or rounds other values in their place, can miss the bound.
Values may be sent and summed in bfloat16 or wider, within the bound.
A program may use at most 64 MiB of HBM per device.

```python
import jax
import jax.numpy as jnp
from jax import lax

MODEL_WIDTH = 4096
QUERY_HEADS = 16
KEY_VALUE_HEADS = 4
HEAD_SIZE = 128
LENGTH = 2048


def draw_tokens(key, part):
    rows = LENGTH
    base = jnp.clip(jax.random.normal(jax.random.fold_in(key, 1), (rows, MODEL_WIDTH), jnp.float32), -6.0, 6.0)
    return base.astype(jnp.bfloat16)


def steps_of(own_key, shape, shards, low, top_value):
    factor_of = 1.0
    for axis_at, blocks in shards:
        draws = jax.random.uniform(jax.random.fold_in(jax.random.fold_in(own_key, 6), axis_at), (blocks,), jnp.float32, low / len(shards), top_value / len(shards))
        factor_of = factor_of * jnp.repeat(jnp.exp(draws), shape[axis_at] // blocks).reshape((-1,) + (1,) * (len(shape) - 1 - axis_at))
    return factor_of


def noise(own_key, dims, deviation, most, cuts=(), kind=jnp.bfloat16):
    entries = deviation * jax.random.normal(own_key, dims, jnp.float32)
    if cuts:
        entries = entries * steps_of(own_key, dims, cuts, -0.22, 0.18)
    return jnp.clip(entries, -most, most).astype(kind)


def setup_inputs(seed: int = 0) -> dict:
    arg_keys = jax.random.split(jax.random.key(seed), 6)
    tokens = draw_tokens(jax.random.fold_in(arg_keys[5], 71), 0)
    w_query = noise(arg_keys[1], (MODEL_WIDTH, QUERY_HEADS * HEAD_SIZE), (MODEL_WIDTH // 4) ** -0.5, 0.1875, ((1, 4),))
    key_matrix = noise(arg_keys[2], (MODEL_WIDTH, KEY_VALUE_HEADS * HEAD_SIZE), MODEL_WIDTH ** -0.5, 0.09375, ((1, 4),))
    value_matrix = noise(arg_keys[3], (MODEL_WIDTH, KEY_VALUE_HEADS * HEAD_SIZE), MODEL_WIDTH ** -0.5, 0.09375, ((1, 4),))
    w_output = noise(arg_keys[4], (QUERY_HEADS * HEAD_SIZE, MODEL_WIDTH), (QUERY_HEADS * HEAD_SIZE) ** -0.5, 0.125, ((0, 4),))
    return {"tokens": tokens, "w_query": w_query, "key_matrix": key_matrix, "value_matrix": value_matrix, "w_output": w_output}


neg_large = -1.0e30


def reference(tokens, w_query, key_matrix, value_matrix, w_output):
    query = jnp.dot(tokens, w_query, preferred_element_type=jnp.float32).astype(jnp.bfloat16)
    keys = jnp.dot(tokens, key_matrix, preferred_element_type=jnp.float32).astype(jnp.bfloat16)
    values = jnp.dot(tokens, value_matrix, preferred_element_type=jnp.float32).astype(jnp.bfloat16)
    query_group = QUERY_HEADS // KEY_VALUE_HEADS
    scale = HEAD_SIZE ** -0.5
    block = min(512, LENGTH)
    blocks = LENGTH // block
    positions = jnp.arange(LENGTH, dtype=jnp.int32)

    def head_cluster(index):
        key_head = lax.dynamic_slice_in_dim(keys, index * HEAD_SIZE, HEAD_SIZE, 1).astype(jnp.float32)
        value_head = lax.dynamic_slice_in_dim(values, index * HEAD_SIZE, HEAD_SIZE, 1).astype(jnp.float32)
        query_heads = lax.dynamic_slice_in_dim(query, index * query_group * HEAD_SIZE, query_group * HEAD_SIZE, 1).reshape(LENGTH, query_group, HEAD_SIZE)

        def query_block(block_index):
            first = block_index * block
            piece = lax.dynamic_slice_in_dim(query_heads, first, block, 0).astype(jnp.float32)
            scores = jnp.einsum("qgd,td->gqt", piece, key_head) * scale
            query_places = first + jnp.arange(block, dtype=jnp.int32)
            allowed = positions[None, :] <= query_places[:, None]
            top = jnp.max(jnp.where(allowed, scores, neg_large), axis=-1)
            weights = jnp.where(allowed, jnp.exp(scores - top[..., None]), 0.0)
            total = jnp.sum(weights, axis=-1)
            rounded = lax.optimization_barrier(weights.astype(jnp.bfloat16))
            summed = jnp.einsum("gqt,td->gqd", rounded.astype(jnp.float32), value_head)
            return (summed / total[..., None]).astype(jnp.bfloat16)

        output = lax.map(query_block, jnp.arange(blocks, dtype=jnp.int32))
        return output.transpose(0, 2, 1, 3).reshape(LENGTH, query_group * HEAD_SIZE)

    head_list = lax.map(head_cluster, jnp.arange(KEY_VALUE_HEADS, dtype=jnp.int32))
    attended = head_list.transpose(1, 0, 2).reshape(LENGTH, QUERY_HEADS * HEAD_SIZE)
    return jnp.dot(attended, w_output, preferred_element_type=jnp.float32).astype(jnp.bfloat16)
```

```python
import functools
import math

import jax
import jax.numpy as jnp
from jax import lax
from jax.experimental import pallas as pl
from jax.experimental.pallas import tpu as pltpu
from jax.sharding import PartitionSpec as P

MESH = pl.DeviceIdType.MESH
PIECES = (2, 2, 2, 1, 1)
CROSSING = (4,)
LONG_PIECES = (1, 1, 1, 1)
STEP = 64
LANES = 128
UNROLLED = 4
NEG_LARGE = -1e30

scope = jax.named_scope


def layer_kernel(n_ctx, n_head, lengths, crossing, early, *refs):
    pieces = len(lengths)
    tokens, wq_hbm, wk_hbm, wv_hbm, wo_hbm, out = refs[:6]
    weights, wo, tok, partial, query, top_ref, att_own, att_pair = refs[6:14]
    own_sum, far_send, far_part, result = refs[14:18]
    kv = refs[18 : 18 + pieces]
    scores = refs[18 + pieces : 18 + 2 * pieces]
    (
        w_sem,
        own_sem,
        pair_send,
        pair_recv,
        wo_sem,
        wo_send,
        wo_recv,
        t_send,
        t_recv,
        kv_direct,
        kv_cross,
        kv_pair,
        kv_recv,
        a_send,
        a_recv,
        r_send,
        r_recv,
        o_sem,
    ) = refs[18 + 2 * pieces :]
    rows, depth = tokens.shape
    size = wk_hbm.shape[1]
    heads = wq_hbm.shape[1]
    group = heads // size
    chunks, step = own_sum.shape[:2]
    starts = [sum(lengths[:index]) for index in range(pieces)]
    c = lax.axis_index("ctx")
    h = lax.axis_index("head")
    place, side = c // 2, c % 2
    core = h % 2
    pair = h + 1 - 2 * core
    across = (h + 2) % n_head
    diag = across + 1 - 2 * core
    ctx_pair = c + 1 - 2 * side
    columns = n_ctx // 2
    later = columns - 1 - place
    last = pieces - 1
    ahead = last - 1
    f32, bf16 = jnp.float32, jnp.bfloat16

    def remote(src, dst, send, recv, target):
        return pltpu.make_async_remote_copy(
            src_ref=src,
            dst_ref=dst,
            send_sem=send,
            recv_sem=recv,
            device_id=target,
            device_id_type=MESH,
        )

    def block(index, count):
        return pl.ds(pl.multiple_of(index * count, count), count)

    def part(k):
        return block(k, step)

    def piece(k):
        return pl.ds(starts[k], lengths[k])

    for k in range(pieces):
        if (2 * lengths[k]) % LANES:
            kv[k][...] = jnp.zeros(kv[k].shape, bf16)

    own_load = pltpu.make_async_copy(tokens, tok.at[0], own_sem)
    own_load.start()
    barrier = pltpu.get_barrier_semaphore()
    for shift in range(1, columns):
        other = ((place + shift) % columns) * 2 + side
        pl.semaphore_signal(barrier, inc=1, device_id={"ctx": other}, device_id_type=MESH)
        if crossing:
            other = other + 1 - 2 * side
            pl.semaphore_signal(barrier, inc=1, device_id={"ctx": other}, device_id_type=MESH)
    pl.semaphore_signal(barrier, inc=1, device_id={"ctx": ctx_pair}, device_id_type=MESH)
    for other in (pair, across):
        pl.semaphore_signal(barrier, inc=1, device_id={"head": other}, device_id_type=MESH)

    with scope("own"):
        own_load.wait()
    loads = []
    for slot, owner in enumerate((h, pair, across, diag)):
        at = block(owner, depth)
        into = weights.at[slot]
        loads.append(
            (
                pltpu.make_async_copy(
                    wk_hbm.at[at], into.at[:, pl.ds(0, size)], w_sem.at[slot, 0]
                ),
                pltpu.make_async_copy(
                    wv_hbm.at[at], into.at[:, pl.ds(size, size)], w_sem.at[slot, 1]
                ),
                pltpu.make_async_copy(
                    wq_hbm.at[at], into.at[:, pl.ds(2 * size, heads)], w_sem.at[slot, 2]
                ),
            )
        )
        for load in loads[-1]:
            load.start()
    with scope("barrier"):
        pl.semaphore_wait(barrier, 2 + columns + (columns - 1 if crossing else 0))

    def token_copy(k):
        return remote(
            tok.at[0, piece(k)],
            tok.at[2, piece(k)],
            t_send.at[0, k],
            t_recv.at[0, k],
            {"head": across},
        )

    def token_relay(k):
        return remote(
            tok.at[2, piece(k)],
            tok.at[3, piece(k)],
            t_send.at[1, k],
            t_recv.at[1, k],
            {"head": pair},
        )

    for k in range(pieces):
        token_copy(k).start()
    pair_tokens = remote(tok.at[0], tok.at[1], pair_send, pair_recv, {"head": pair})
    pair_tokens.start()

    wo_loads = [
        pltpu.make_async_copy(
            wo_hbm.at[:, block(owner, depth)], wo.at[slot, 0], wo_sem.at[slot]
        )
        for slot, owner in enumerate((h, across))
    ]
    wo_copies = [
        remote(
            wo_hbm.at[:, block(owner, depth)],
            wo.at[slot, 1],
            wo_send.at[slot],
            wo_recv.at[slot],
            {"head": pair},
        )
        for slot, owner in enumerate((pair, diag))
    ]

    def kv_copy(which, k, sem, target):
        return remote(
            kv[k].at[which], kv[k].at[which], sem, kv_recv.at[which, k], {"ctx": target}
        )

    def direct_copy(shift, k):
        return kv_copy(c, k, kv_direct.at[shift, k], c + 2 * shift)

    def cross_copy(shift, k):
        return kv_copy(c, k, kv_cross.at[shift, k], ctx_pair + 2 * shift)

    def pair_copy(where, k):
        return kv_copy(2 * where + side, k, kv_pair.at[where, k], ctx_pair)

    def relay(k):
        def one(index, carry):
            where = place - 1 - index
            pair_copy(where, k).wait_recv()
            if k not in crossing:
                pair_copy(where, k).start()
            return carry

        with scope(f"relay{k}"):
            lax.fori_loop(0, place, one, 0)

    def arrive(k):
        def one(where, carry):
            kv_copy(2 * where + 1 - side, k, kv_pair.at[where, k], ctx_pair).wait_recv()
            return carry

        with scope(f"arrive{k}"):
            lax.fori_loop(0, place + 1, one, 0)

    shared, queries_at = pl.ds(0, 2 * size), pl.ds(2 * size, heads)

    def term(slot, at, wanted):
        return jnp.dot(
            tok[slot, at, :], weights[slot, :, wanted], preferred_element_type=f32
        )

    def begin():
        every = slice(None)
        for load in loads[0]:
            load.wait()
        partial[...] = term(0, every, every)
        pair_tokens.wait_recv()
        for load in loads[1]:
            load.wait()
        partial[...] += term(1, every, every)
        for load in loads[2] + loads[3]:
            load.wait()
        for copy in wo_loads + wo_copies:
            copy.start()

    def add_across(k):
        with scope(f"across{k}"):
            token_copy(k).wait_recv()
        token_relay(k).start()
        partial[piece(k), :] += term(2, piece(k), slice(None))

    def finish_keys(k):
        with scope(f"diag{k}"):
            token_relay(k).wait_recv()
        kv[k][c] = (partial[piece(k), shared] + term(3, piece(k), shared)).astype(bf16)

        def send(index, carry):
            direct_copy(later - index, k).start()
            if k in crossing:
                cross_copy(later - index, k).start()
            return carry

        lax.fori_loop(0, later, send, 0)
        pair_copy(place, k).start()

    def finish_queries(k):
        found = partial[piece(k), queries_at] + term(3, piece(k), queries_at)
        for g in range(group):
            query[g, piece(k), :] = found[:, g * size : (g + 1) * size].astype(bf16)

    with scope("begin"):
        begin()
    for k in range(pieces):
        add_across(k)
        if k > 0:
            finish_queries(k - 1)
        finish_keys(k)
        if 0 < k < last - 1:
            relay(k - 1)
    finish_queries(last)
    relay(last - 2)
    relay(last - 1)

    tall = group * step
    factor = (size ** (-0.5)) * math.log2(math.e)

    def fold(values, op):
        result = values[:, :LANES]
        for index in range(1, values.shape[1] // LANES):
            result = op(result, values[:, index * LANES : (index + 1) * LANES])
        return result

    def queries_of(k):
        return query[:, part(k), :].reshape(tall, size)

    def product(queries, keys):
        return lax.dot_general(
            queries, keys, (((1,), (1,)), ((), ())), preferred_element_type=f32
        )

    def mask(found, k, j, first):
        width = found.shape[1]
        column = lax.broadcasted_iota(jnp.int32, (step, width), 1)
        shift = lengths[j].bit_length() - 1
        at_key = (column >> shift) * rows + (column & (lengths[j] - 1)) + starts[j]
        at_query = lax.broadcasted_iota(jnp.int32, (step, width), 0) + k * step
        allowed = at_key <= at_query + (side - first) * rows
        return jnp.where(jnp.concatenate([allowed] * group, axis=0), found, NEG_LARGE)

    def span(count, j):
        width = 2 * (count + 1) * lengths[j]
        width += -width % LANES
        begin = 2 * count * lengths[j]
        begin -= begin % LANES
        return width, width // lengths[j], begin

    def keys_of(j, blocks):
        return kv[j][pl.ds(0, blocks), :, pl.ds(0, size)].reshape(-1, size)

    def values_of(j, blocks):
        return kv[j][pl.ds(0, blocks), :, pl.ds(size, size)].reshape(-1, size)

    def score(k, j, count):
        width, blocks, begin = span(count, j)
        found = product(queries_of(k), keys_of(j, blocks))
        tail = mask(found[:, begin:], k, j, begin // lengths[j] - 2 * count)
        scores[j][k, :, pl.ds(begin, width - begin)] = tail
        top = fold(tail, jnp.maximum)
        if begin:
            scores[j][k, :, pl.ds(0, begin)] = found[:, :begin]
            top = jnp.maximum(top, fold(found[:, :begin], jnp.maximum))
        return top

    def prepare(count, k, carry):
        top_ref[k] = functools.reduce(
            jnp.maximum, [score(k, j, count) for j in range(ahead)]
        )
        return carry

    def weigh(found, top, values, state):
        total, summed = state
        weighed = jnp.exp2((found - top) * factor)
        summed = summed + jnp.dot(weighed.astype(bf16), values, preferred_element_type=f32)
        return total + fold(weighed, jnp.add), summed

    def close(k, state):
        total, summed = state
        total = jnp.sum(total, axis=-1, keepdims=True)
        mixed = (summed / total).astype(bf16)
        for g in range(group):
            att_own[k, :, pl.ds(g * size, size)] = mixed[g * step : (g + 1) * step]

    nothing = (jnp.zeros((tall, LANES), f32), jnp.zeros((tall, size), f32))

    def attention(k, count):
        top = top_ref[k]
        for j in range(ahead, pieces):
            top = jnp.maximum(top, score(k, j, count))
        top = jnp.max(top, axis=-1, keepdims=True)
        state = nothing
        for j in range(pieces):
            width, blocks, _ = span(count, j)
            state = weigh(
                scores[j][k, :, pl.ds(0, width)], top, values_of(j, blocks), state
            )
        close(k, state)

    def attention_at_length(k):
        queries = queries_of(k)

        def pick(j, where, at):
            return kv[j][pl.ds(2 * where, 2), :, pl.ds(at, size)].reshape(-1, size)

        top = jnp.full((tall, LANES), NEG_LARGE, f32)
        for j in range(pieces):

            def first_pass(where, top, j=j):
                found = product(queries, pick(j, where, 0))
                scores[j][where] = found
                return jnp.maximum(top, fold(found, jnp.maximum))

            found = mask(product(queries, pick(j, place, 0)), k, j, 0)
            scores[j][place] = found
            top = jnp.maximum(top, fold(found, jnp.maximum))
            top = lax.fori_loop(0, place, first_pass, top)
        top = jnp.max(top, axis=-1, keepdims=True)
        state = nothing
        for j in range(pieces):

            def second_pass(where, state, j=j):
                return weigh(scores[j][where], top, pick(j, where, size), state)

            state = lax.fori_loop(0, place + 1, second_pass, state)
        close(k, state)

    def at_place(call):
        for count in range(columns):
            pl.when(place == count)(functools.partial(call, count))

    def prepare_some(low, high):
        def run(count):
            lax.fori_loop(low, high, functools.partial(prepare, count), 0)

        with scope("prepare"):
            at_place(run)

    for j in range(ahead):
        arrive(j)
    if early:
        prepare_some(0, chunks // 2)
        relay(last)
        prepare_some(chunks // 2, chunks)
    else:
        relay(last)
    for j in range(ahead, pieces):
        arrive(j)

    with scope("wo"):
        for load in wo_loads:
            load.wait()
        for copy in wo_copies:
            copy.wait_recv()

    def att_copy(k):
        return remote(
            att_own.at[k], att_pair.at[k], a_send.at[k], a_recv.at[k], {"head": pair}
        )

    def far_copy(k):
        return remote(
            far_send.at[k], far_part.at[k], r_send.at[k], r_recv.at[k], {"head": across}
        )

    def attend(k):
        with scope("attention"):
            if early:
                at_place(functools.partial(attention, k))
            else:
                attention_at_length(k)
        att_copy(k).start()

    def mix(k, slot):
        return jnp.dot(att_own[k], wo[slot, 0], preferred_element_type=f32) + jnp.dot(
            att_pair[k], wo[slot, 1], preferred_element_type=f32
        )

    def share(k):
        own_sum[k] = jnp.dot(att_own[k], wo[1, 0], preferred_element_type=f32)
        with scope("exchange"):
            att_copy(k).wait_recv()
        with scope("mix"):
            from_pair = jnp.dot(att_pair[k], wo[1, 1], preferred_element_type=f32)
            far_send[k] = (own_sum[k] + from_pair).astype(bf16)
            far_copy(k).start()
            own_sum[k] = mix(k, 0)

    def both(k, carry):
        attend(k)
        share(k)
        return carry

    lax.fori_loop(0, chunks, both, 0)

    def out_copy(k):
        return pltpu.make_async_copy(result.at[k], out.at[part(k)], o_sem.at[k])

    def finish(k, carry):
        with scope("far"):
            far_copy(k).wait_recv()
        result[k] = (own_sum[k] + far_part[k].astype(f32)).astype(bf16)
        out_copy(k).start()
        return carry

    lax.fori_loop(0, chunks, finish, 0)

    pair_tokens.wait_send()
    for copy in wo_copies:
        copy.wait_send()
    for k in range(pieces):
        token_copy(k).wait_send()
        token_relay(k).wait_send()

    def sent(index, carry):
        for k in range(pieces):
            direct_copy(later - index, k).wait_send()
            if k in crossing:
                cross_copy(later - index, k).wait_send()
        return carry

    lax.fori_loop(0, later, sent, 0)

    def passed(where, carry):
        for k in range(pieces):
            if k not in crossing:
                pair_copy(where, k).wait_send()
        return carry

    lax.fori_loop(0, place, passed, 0)
    for k in range(pieces):
        pair_copy(place, k).wait_send()

    def closed(k, carry):
        att_copy(k).wait_send()
        far_copy(k).wait_send()
        out_copy(k).wait()
        return carry

    with scope("out"):
        lax.fori_loop(0, chunks, closed, 0)


def solution(mesh):
    n_ctx, n_head = mesh.shape["ctx"], mesh.shape["head"]

    def local(tokens, w_query, key_matrix, value_matrix, w_output):
        rows, depth = tokens.shape
        width, size = key_matrix.shape
        heads = w_query.shape[1]
        group = heads // size
        chunks = rows // STEP
        columns = n_ctx // 2
        early = columns <= UNROLLED
        shares = PIECES if early else LONG_PIECES
        crossing = CROSSING if early else ()
        lengths = [count * rows // sum(shares) for count in shares]
        pieces = len(lengths)
        tall = group * STEP
        bf16, f32 = jnp.bfloat16, jnp.float32
        dma = pltpu.SemaphoreType.DMA
        vmem = pltpu.VMEM

        def keys(length):
            return vmem((n_ctx + -n_ctx % max(LANES // length, 1), length, 2 * size), bf16)

        def found(length):
            if early:
                total = n_ctx * length
                return vmem((chunks, tall, total + -total % LANES), f32)
            return vmem((columns, tall, 2 * length), f32)

        hbm = pl.BlockSpec(memory_space=pltpu.HBM)
        return pl.pallas_call(
            functools.partial(layer_kernel, n_ctx, n_head, lengths, crossing, early),
            out_shape=jax.ShapeDtypeStruct((rows, depth), bf16),
            in_specs=[hbm] * 5,
            out_specs=hbm,
            scratch_shapes=[
                vmem((n_head, depth, 2 * size + heads), bf16),
                vmem((2, 2, heads, depth), bf16),
                vmem((n_head, rows, depth), bf16),
                vmem((rows, 2 * size + heads), f32),
                vmem((group, rows, size), bf16),
                vmem((chunks, tall, LANES), f32),
                vmem((chunks, STEP, heads), bf16),
                vmem((chunks, STEP, heads), bf16),
                vmem((chunks, STEP, depth), f32),
                vmem((chunks, STEP, depth), bf16),
                vmem((chunks, STEP, depth), bf16),
                vmem((chunks, STEP, depth), bf16),
                *[keys(length) for length in lengths],
                *[found(length) for length in lengths],
                dma((n_head, 3)),
                dma,
                dma,
                dma,
                dma((2,)),
                dma((2,)),
                dma((2,)),
                dma((2, pieces)),
                dma((2, pieces)),
                dma((columns, pieces)),
                dma((columns, pieces)),
                dma((columns, pieces)),
                dma((n_ctx, pieces)),
                dma((chunks,)),
                dma((chunks,)),
                dma((chunks,)),
                dma((chunks,)),
                dma((chunks,)),
            ],
            compiler_params=pltpu.CompilerParams(
                collective_id=0,
                has_side_effects=True,
                vmem_limit_bytes=60 * 1024 * 1024,
            ),
        )(tokens, w_query, key_matrix, value_matrix, w_output)

    return jax.shard_map(
        local,
        mesh=mesh,
        in_specs=(
            P("ctx", "head"),
            P(None, "head"),
            P(None, "head"),
            P(None, "head"),
            P("head", None),
        ),
        out_specs=P("ctx", "head"),
        check_vma=False,
    )
```

```python
import functools
import math

import jax
import jax.numpy as jnp
from jax import lax
from jax.experimental import pallas as pl
from jax.experimental.pallas import tpu as pltpu
from jax.sharding import PartitionSpec as P

MESH = pl.DeviceIdType.MESH
SHORT_GROUPS = ((1, 1, 1, 1), (1, 1), (1, 1))
LONG_GROUPS = ((2,), (2,), (2,), (2,))
CROSSING = (7,)
FLYING = 4
LAG = 3
STEP = 64
LANES = 128
UNROLLED = 4
NEG_LARGE = -1e30

scope = jax.named_scope


def layer_kernel(n_ctx, n_head, shares, early, *refs):
    groups = len(shares)
    tokens, wq_hbm, wk_hbm, wv_hbm, wo_hbm, out = refs[:6]
    weights, wo, tok, partial, query, top_ref, att_own, att_pair = refs[6:14]
    own_sum, far_send, far_part = refs[14:17]
    kv = refs[17 : 17 + groups]
    scores = refs[17 + groups : 17 + 2 * groups]
    (
        w_sem,
        wo_sem,
        tok_sem,
        t_send,
        across_recv,
        diag_recv,
        direct_send,
        pair_send,
        cross_send,
        same_recv,
        other_recv,
        a_send,
        a_recv,
        r_send,
        r_recv,
    ) = refs[17 + 2 * groups :]
    rows, depth = tokens.shape
    size = wk_hbm.shape[1]
    heads = wq_hbm.shape[1]
    group = heads // size
    c = lax.axis_index("ctx")
    h = lax.axis_index("head")
    place, side = c // 2, c % 2
    core = h % 2
    pair = h + 1 - 2 * core
    across = (h + 2) % n_head
    diag = across + 1 - 2 * core
    ctx_pair = c + 1 - 2 * side
    columns = n_ctx // 2
    later = columns - 1 - place
    at_end = later == 0
    f32, bf16 = jnp.float32, jnp.bfloat16
    every = slice(None)

    unit = rows // sum(sum(share) for share in shares)
    lengths, starts, owners, offsets, first_row = [], [], [], [], []
    row = 0
    for g, share in enumerate(shares):
        first_row.append(row)
        for count in share:
            owners.append(g)
            starts.append(row)
            offsets.append(row - first_row[g])
            lengths.append(count * unit)
            row += count * unit
    pieces = len(lengths)
    sizes = [sum(share) * unit for share in shares]
    last = pieces - 1
    crossing = CROSSING if early else ()

    def remote(src, dst, send, recv, target):
        return pltpu.make_async_remote_copy(
            src_ref=src,
            dst_ref=dst,
            send_sem=send,
            recv_sem=recv,
            device_id=target,
            device_id_type=MESH,
        )

    def sent(ref, sem):
        remote(ref, ref, sem, sem, {"head": pair}).wait_send()

    def came(ref, sem):
        remote(ref, ref, sem, sem, {"head": pair}).wait_recv()

    def block(index, count):
        return pl.ds(pl.multiple_of(index * count, count), count)

    def piece(k):
        return pl.ds(starts[k], lengths[k])

    own_load = pltpu.make_async_copy(tokens, tok.at[0], tok_sem.at[0])
    own_load.start()
    barrier = pltpu.get_barrier_semaphore()

    def greet(target):
        pl.semaphore_signal(barrier, inc=1, device_id=target, device_id_type=MESH)

    for shift in range(1, columns):
        other = ((place + shift) % columns) * 2 + side
        greet({"ctx": other})
        if early:
            greet({"ctx": other + 1 - 2 * side})
    greet({"ctx": ctx_pair})
    greet({"head": pair})
    greet({"head": across})
    with scope("own"):
        own_load.wait()
    for slot, owner in enumerate((h, pair, across, diag)):
        at = block(owner, depth)
        into = weights.at[slot]
        for src, low, width in (
            (wk_hbm, 0, size),
            (wv_hbm, size, size),
            (wq_hbm, 2 * size, heads),
        ):
            pltpu.make_async_copy(
                src.at[at], into.at[:, pl.ds(low, width)], w_sem.at[slot]
            ).start()

    def loaded(slot):
        pltpu.make_async_copy(weights.at[slot], weights.at[slot], w_sem.at[slot]).wait()

    with scope("barrier"):
        pl.semaphore_wait(barrier, 2 + columns + (columns - 1 if early else 0))

    def token_copy(k):
        return remote(
            tok.at[0, piece(k)],
            tok.at[2, piece(k)],
            t_send.at[0],
            across_recv.at[k],
            {"head": across},
        )

    def token_relay(k):
        return remote(
            tok.at[2, piece(k)],
            tok.at[3, piece(k)],
            t_send.at[1],
            diag_recv.at[k],
            {"head": pair},
        )

    for k in range(min(FLYING, pieces)):
        token_copy(k).start()
    pair_tokens = remote(tok.at[0], tok.at[1], tok_sem.at[1], tok_sem.at[2], {"head": pair})
    pair_tokens.start()

    def fetch_output_weights():
        for slot, owner in enumerate((h, across)):
            pltpu.make_async_copy(
                wo_hbm.at[:, block(owner, depth)], wo.at[0, slot], wo_sem.at[0]
            ).start()
        for slot, owner in enumerate((pair, diag)):
            remote(
                wo_hbm.at[:, block(owner, depth)],
                wo.at[1, slot],
                wo_sem.at[1],
                wo_sem.at[2],
                {"head": pair},
            ).start()

    def kv_copy(which, k, send, recv, target):
        at = kv[owners[k]].at[which, pl.ds(offsets[k], lengths[k])]
        return remote(at, at, send, recv, {"ctx": target})

    def direct_copy(shift, k):
        return kv_copy(c, k, direct_send.at[shift], same_recv.at[place, k], c + 2 * shift)

    def cross_copy(shift, k):
        sem = cross_send.at[shift, int(k in crossing)]
        target = ctx_pair + 2 * shift
        return kv_copy(c, k, sem, other_recv.at[place, owners[k]], target)

    def pair_copy(where, k):
        sem = pair_send.at[where, int(k in crossing)]
        recv = other_recv.at[where, owners[k]]
        return kv_copy(2 * where + side, k, sem, recv, ctx_pair)

    def same_arrived(where, k):
        at = kv[owners[k]].at[2 * where + side, pl.ds(offsets[k], lengths[k])]
        came(at, same_recv.at[where, k])

    def relayed(k):
        if k in crossing:
            return 0
        return jnp.where(at_end, place - 1, place) if early else place

    def relay(k):
        def one(where, carry):
            same_arrived(where, k)
            pair_copy(where, k).start()
            return carry

        with scope(f"relay{k}"):
            lax.fori_loop(0, relayed(k), one, 0)

    def arrive(g):
        def other(where, carry):
            came(kv[g].at[2 * where + 1 - side], other_recv.at[where, g])
            return carry

        with scope(f"arrive{g}"):
            for k in range(pieces):
                if owners[k] == g:

                    def same(where, carry, k=k):
                        same_arrived(where, k)
                        return carry

                    lax.fori_loop(relayed(k), place, same, 0)
            lax.fori_loop(0, place + 1, other, 0)

    shared, queries_at = pl.ds(0, 2 * size), pl.ds(2 * size, heads)

    def term(slot, at, wanted):
        return jnp.dot(
            tok[slot, at, :], weights[slot, :, wanted], preferred_element_type=f32
        )

    def begin():
        loaded(0)
        partial[...] = term(0, every, every)
        pair_tokens.wait_recv()
        loaded(1)
        partial[...] += term(1, every, every)
        loaded(2)
        loaded(3)
        fetch_output_weights()

    def add_across(k):
        with scope(f"across{k}"):
            token_copy(k).wait_recv()
        token_relay(k).start()
        if k + FLYING < pieces:
            token_copy(k + FLYING).start()
        partial[piece(k), :] += term(2, piece(k), every)

    def finish_keys(k):
        with scope(f"diag{k}"):
            token_relay(k).wait_recv()
        found = partial[piece(k), shared] + term(3, piece(k), shared)
        kv[owners[k]][c, pl.ds(offsets[k], lengths[k]), :] = found.astype(bf16)

        def send(index, carry):
            direct_copy(later - index, k).start()
            if k in crossing:
                cross_copy(later - index, k).start()
            return carry

        lax.fori_loop(0, later, send, 0)
        if early and k not in crossing:

            @pl.when(later == 1)
            def _():
                cross_copy(1, k).start()

        pair_copy(place, k).start()

    def finish_queries(at):
        found = partial[at, queries_at] + term(3, at, queries_at)
        for g in range(group):
            query[g, at, :] = found[:, g * size : (g + 1) * size].astype(bf16)

    with scope("begin"):
        begin()
    done = 0
    for k in range(pieces):
        add_across(k)
        if starts[k] - done >= STEP:
            finish_queries(pl.ds(done, starts[k] - done))
            done = starts[k]
        finish_keys(k)
        if k >= LAG:
            relay(k - LAG)
    finish_queries(pl.ds(done, rows - done))
    waiting = list(range(max(pieces - LAG, 0), pieces))

    factor = (size ** (-0.5)) * math.log2(math.e)

    def fold(values, op):
        result = values[:, :LANES]
        for index in range(1, values.shape[1] // LANES):
            result = op(result, values[:, index * LANES : (index + 1) * LANES])
        return result

    def queries_of(at, count):
        return query[:, at, :].reshape(group * count, size)

    def product(queries, keys):
        return lax.dot_general(
            queries, keys, (((1,), (1,)), ((), ())), preferred_element_type=f32
        )

    def mask(found, low, count, g):
        width = found.shape[1]
        column = lax.broadcasted_iota(jnp.int32, (count, width), 1)
        shift = sizes[g].bit_length() - 1
        at_key = (column >> shift) * rows + (column & (sizes[g] - 1)) + first_row[g]
        at_query = lax.broadcasted_iota(jnp.int32, (count, width), 0) + low
        allowed = at_key <= at_query + side * rows
        return jnp.where(jnp.concatenate([allowed] * group, axis=0), found, NEG_LARGE)

    def keys_of(g, where, places):
        return kv[g][pl.ds(2 * where, 2 * places), :, pl.ds(0, size)].reshape(-1, size)

    def values_of(g, where, places):
        return kv[g][pl.ds(2 * where, 2 * places), :, pl.ds(size, size)].reshape(-1, size)

    def score(at, low, count, g, before):
        found = product(queries_of(at, count), keys_of(g, 0, before + 1))
        split = 2 * before * sizes[g]
        tail = mask(found[:, split:], low, count, g)
        scores[g][:, at, pl.ds(split, 2 * sizes[g])] = tail.reshape(group, count, -1)
        top = fold(tail, jnp.maximum)
        if split:
            head = found[:, :split]
            scores[g][:, at, pl.ds(0, split)] = head.reshape(group, count, split)
            top = jnp.maximum(top, fold(head, jnp.maximum))
        return top

    def weigh(found, top, values, state):
        total, summed = state
        weighed = jnp.exp2((found - top) * factor)
        summed = summed + jnp.dot(weighed.astype(bf16), values, preferred_element_type=f32)
        return total + fold(weighed, jnp.add), summed

    def close(at, count, state):
        total, summed = state
        total = jnp.sum(total, axis=-1, keepdims=True)
        mixed = (summed / total).astype(bf16)
        for g in range(group):
            att_own[at, pl.ds(g * size, size)] = mixed[g * count : (g + 1) * count]

    def nothing(count):
        return tuple(jnp.zeros((group * count, width), f32) for width in (LANES, size))

    def attention(at, low, count, before):
        top = top_ref[:, at, :].reshape(group * count, LANES)
        top = jnp.maximum(top, score(at, low, count, groups - 1, before))
        top = jnp.max(top, axis=-1, keepdims=True)
        state = nothing(count)
        for g in range(groups):
            width = 2 * (before + 1) * sizes[g]
            found = scores[g][:, at, pl.ds(0, width)].reshape(group * count, width)
            state = weigh(found, top, values_of(g, 0, before + 1), state)
        close(at, count, state)

    def attention_at_length(at, low, count):
        queries = queries_of(at, count)
        here = pl.ds(0, group * count)
        top = jnp.full((group * count, LANES), NEG_LARGE, f32)
        for g in range(groups):

            def first_pass(where, top, g=g):
                found = product(queries, keys_of(g, where, 1))
                scores[g][where, here] = found
                return jnp.maximum(top, fold(found, jnp.maximum))

            found = mask(product(queries, keys_of(g, place, 1)), low, count, g)
            scores[g][place, here] = found
            top = jnp.maximum(top, fold(found, jnp.maximum))
            top = lax.fori_loop(0, place, first_pass, top)
        top = jnp.max(top, axis=-1, keepdims=True)
        state = nothing(count)
        for g in range(groups):

            def second_pass(where, state, g=g):
                return weigh(scores[g][where, here], top, values_of(g, where, 1), state)

            state = lax.fori_loop(0, place + 1, second_pass, state)
        close(at, count, state)

    def at_place(call):
        for before in range(columns):
            pl.when(place == before)(functools.partial(call, before))

    def prepare(g):
        count = min(2 * STEP, rows)

        def run(before):
            def one(index, carry):
                at = block(index, count)
                top = score(at, index * count, count, g, before)
                top = top.reshape(group, count, LANES)
                if g > 0:
                    top = jnp.maximum(top, top_ref[:, at, :])
                top_ref[:, at, :] = top
                return carry

            lax.fori_loop(0, rows // count, one, 0)

        with scope(f"prepare{g}"):
            at_place(run)

    for k in waiting[:-2]:
        relay(k)
    if early:
        arrive(0)
        prepare(0)
        for k in waiting[-2:]:
            relay(k)
        for g in range(1, groups - 1):
            arrive(g)
            prepare(g)
        arrive(groups - 1)
    else:
        for k in waiting[-2:]:
            relay(k)
        for g in range(groups):
            arrive(g)

    with scope("wo"):
        pltpu.make_async_copy(wo.at[0], wo.at[0], wo_sem.at[0]).wait()
        came(wo.at[1], wo_sem.at[2])

    chunks = [(0, STEP // 2), (STEP // 2, STEP // 2)]
    chunks += [(low, STEP) for low in range(STEP, rows, STEP)]

    def att_copy(k, at):
        return remote(
            att_own.at[at], att_pair.at[at], a_send, a_recv.at[k], {"head": pair}
        )

    def far_copy(k, at):
        return remote(
            far_send.at[at], far_part.at[at], r_send, r_recv.at[k], {"head": across}
        )

    def attend(k, at, low, count):
        with scope("attention"):
            if early:
                at_place(functools.partial(attention, at, low, count))
            else:
                attention_at_length(at, low, count)
        att_copy(k, at).start()

    def mix(ref, at, source, slot):
        return jnp.dot(ref[at, :], wo[source, slot], preferred_element_type=f32)

    def share(k, at):
        own = mix(att_own, at, 0, 1)
        with scope("exchange"):
            att_copy(k, at).wait_recv()
        with scope("mix"):
            far_send[at, :] = (own + mix(att_pair, at, 1, 1)).astype(bf16)
            far_copy(k, at).start()

    def static(k):
        low, count = chunks[k]
        return pl.ds(low, count), low, count

    attend(0, *static(0))
    attend(1, *static(1))
    share(0, static(0)[0])
    full = rows // STEP

    def attend_full(index):
        attend(index + 1, block(index, STEP), index * STEP, STEP)

    if full > 1:
        attend_full(1)
    share(1, static(1)[0])

    def both(index, carry):
        attend_full(index + 1)
        share(index + 1, block(index, STEP))
        return carry

    lax.fori_loop(1, full - 1, both, 0)
    if full > 1:
        share(full, block(full - 1, STEP))
    with scope("keep"):
        own_sum[...] = mix(att_own, every, 0, 0) + mix(att_pair, every, 1, 0)

    for k, (low, count) in enumerate(chunks):
        at = pl.ds(low, count)
        with scope(f"far{k}"):
            far_copy(k, at).wait_recv()
        out[at, :] = (own_sum[at, :] + far_part[at, :].astype(f32)).astype(out.dtype)

    with scope("sent"):
        sent(tok.at[0], tok_sem.at[1])
        sent(tok.at[0], t_send.at[0])
        sent(tok.at[2], t_send.at[1])
        sent(wo.at[1], wo_sem.at[1])
        sent(att_own, a_send)
        sent(far_send, r_send)
        straight = sum(lengths[k] for k in range(pieces) if k not in crossing)
        crossed = rows - straight

        def keys_sent(count, sem):
            sent(far_send.at[pl.ds(0, count), pl.ds(0, 2 * size)], sem)

        def direct_sent(shift, carry):
            keys_sent(rows, direct_send.at[shift])
            if crossed:
                keys_sent(crossed, cross_send.at[shift, 1])
            return carry

        def pair_sent(where, carry):
            keys_sent(straight, pair_send.at[where, 0])
            return carry

        lax.fori_loop(1, later + 1, direct_sent, 0)
        lax.fori_loop(0, relayed(0), pair_sent, 0)
        keys_sent(straight, pair_send.at[place, 0])
        if crossed:
            keys_sent(crossed, pair_send.at[place, 1])
        if early:

            @pl.when(later == 1)
            def _():
                keys_sent(straight, cross_send.at[1, 0])


def solution(mesh):
    n_ctx, n_head = mesh.shape["ctx"], mesh.shape["head"]

    def local(tokens, w_query, key_matrix, value_matrix, w_output):
        rows, depth = tokens.shape
        size = key_matrix.shape[1]
        heads = w_query.shape[1]
        group = heads // size
        columns = n_ctx // 2
        early = columns <= UNROLLED
        shares = SHORT_GROUPS if early else LONG_GROUPS
        unit = rows // sum(sum(share) for share in shares)
        sizes = [sum(share) * unit for share in shares]
        pieces = sum(len(share) for share in shares)
        groups = len(shares)
        chunks = rows // STEP + 1
        bf16, f32 = jnp.bfloat16, jnp.float32
        dma = pltpu.SemaphoreType.DMA
        vmem = pltpu.VMEM

        def found(length):
            if early:
                return vmem((group, rows, n_ctx * length), f32)
            return vmem((columns, group * STEP, 2 * length), f32)

        return pl.pallas_call(
            functools.partial(layer_kernel, n_ctx, n_head, shares, early),
            out_shape=vmem((rows, depth), bf16),
            in_specs=[pl.BlockSpec(memory_space=pltpu.HBM)] * 5,
            out_specs=pl.BlockSpec(memory_space=pltpu.VMEM),
            scratch_shapes=[
                vmem((n_head, depth, 2 * size + heads), bf16),
                vmem((2, 2, heads, depth), bf16),
                vmem((n_head, rows, depth), bf16),
                vmem((rows, 2 * size + heads), f32),
                vmem((group, rows, size), bf16),
                vmem((group, rows, LANES), f32),
                vmem((rows, heads), bf16),
                vmem((rows, heads), bf16),
                vmem((rows, depth), f32),
                vmem((rows, depth), bf16),
                vmem((rows, depth), bf16),
                *[vmem((n_ctx, length, 2 * size), bf16) for length in sizes],
                *[found(length) for length in sizes],
                dma((n_head,)),
                dma((3,)),
                dma((3,)),
                dma((2,)),
                dma((pieces,)),
                dma((pieces,)),
                dma((columns,)),
                dma((columns, 2)),
                dma((columns, 2)),
                dma((columns, pieces)),
                dma((columns, groups)),
                dma,
                dma((chunks,)),
                dma,
                dma((chunks,)),
            ],
            compiler_params=pltpu.CompilerParams(
                collective_id=0,
                has_side_effects=True,
                vmem_limit_bytes=63 * 1024 * 1024,
            ),
        )(tokens, w_query, key_matrix, value_matrix, w_output)

    return jax.shard_map(
        local,
        mesh=mesh,
        in_specs=(
            P("ctx", "head"),
            P(None, "head"),
            P(None, "head"),
            P(None, "head"),
            P("head", None),
        ),
        out_specs=P("ctx", "head"),
        check_vma=False,
    )
```

```python
import functools
import math

import jax
import jax.numpy as jnp
from jax import lax
from jax.experimental import pallas as pl
from jax.experimental.pallas import tpu as pltpu
from jax.sharding import PartitionSpec as P

MESH = pl.DeviceIdType.MESH
SHORT_GROUPS = ((1, 1, 1, 1), (1, 1), (1, 1))
LONG_GROUPS = ((2,), (2,), (2,), (2,))
CROSSING = (7,)
FLYING = 4
LAG = 3
EARLY_SLOTS = 2
STEP = 64
LANES = 128
UNROLLED = 4
NEG_LARGE = -1e30

scope = jax.named_scope


def layer_kernel(n_ctx, n_head, shares, early, *refs):
    groups = len(shares)
    tokens, wq_hbm, wk_hbm, wv_hbm, wo_hbm, out = refs[:6]
    weights, wo, tok, partial, query, top_ref, att_own, att_pair = refs[6:14]
    own_sum, far_send, far_part = refs[14:17]
    kv = refs[17 : 17 + groups]
    scores = refs[17 + groups : 17 + 2 * groups]
    (
        w_sem,
        wo_sem,
        tok_sem,
        across_recv,
        diag_recv,
        kv_send,
        same_recv,
        other_recv,
        a_send,
        a_recv,
        r_recv,
    ) = refs[17 + 2 * groups :]
    rows, depth = tokens.shape
    size = wk_hbm.shape[1]
    heads = wq_hbm.shape[1]
    group = heads // size
    c = lax.axis_index("ctx")
    h = lax.axis_index("head")
    place, side = c // 2, c % 2
    core = h % 2
    pair = h + 1 - 2 * core
    across = (h + 2) % n_head
    diag = across + 1 - 2 * core
    ctx_pair = c + 1 - 2 * side
    columns = n_ctx // 2
    later = columns - 1 - place
    at_end = later == 0
    f32, bf16 = jnp.float32, jnp.bfloat16
    every = slice(None)

    unit = rows // sum(sum(share) for share in shares)
    lengths, starts, owners, offsets, first_row = [], [], [], [], []
    row = 0
    for g, share in enumerate(shares):
        first_row.append(row)
        for count in share:
            owners.append(g)
            starts.append(row)
            offsets.append(row - first_row[g])
            lengths.append(count * unit)
            row += count * unit
    pieces = len(lengths)
    sizes = [sum(share) * unit for share in shares]
    last = pieces - 1
    crossing = CROSSING if early else ()

    def remote(src, dst, send, recv, target):
        return pltpu.make_async_remote_copy(
            src_ref=src,
            dst_ref=dst,
            send_sem=send,
            recv_sem=recv,
            device_id=target,
            device_id_type=MESH,
        )

    def sent(ref, sem):
        remote(ref, ref, sem, sem, {"head": pair}).wait_send()

    def came(ref, sem):
        remote(ref, ref, sem, sem, {"head": pair}).wait_recv()

    def at_place(call):
        for before in range(columns):
            pl.when(place == before)(functools.partial(call, before))

    def block(index, count):
        return pl.ds(pl.multiple_of(index * count, count), count)

    def piece(k):
        return pl.ds(starts[k], lengths[k])

    own_load = pltpu.make_async_copy(tokens, tok.at[0], tok_sem.at[0])
    own_load.start()
    barrier = pltpu.get_barrier_semaphore()

    def greet(target):
        pl.semaphore_signal(barrier, inc=1, device_id=target, device_id_type=MESH)

    for shift in range(1, columns):
        other = ((place + shift) % columns) * 2 + side
        greet({"ctx": other})
        if early:
            greet({"ctx": other + 1 - 2 * side})
    greet({"ctx": ctx_pair})
    greet({"head": pair})
    greet({"head": across})
    with scope("own"):
        own_load.wait()
    def fetch(slot):
        at = block((h, pair, across, diag)[slot], depth)
        into = weights.at[slot]
        for src, low, width in (
            (wk_hbm, 0, size),
            (wv_hbm, size, size),
            (wq_hbm, 2 * size, heads),
        ):
            pltpu.make_async_copy(
                src.at[at], into.at[:, pl.ds(low, width)], w_sem.at[slot]
            ).start()

    def loaded(slot):
        pltpu.make_async_copy(weights.at[slot], weights.at[slot], w_sem.at[slot]).wait()

    for slot in range(EARLY_SLOTS):
        fetch(slot)
    with scope("barrier"):
        pl.semaphore_wait(barrier, 2 + columns + (columns - 1 if early else 0))

    def token_copy(k):
        return remote(
            tok.at[0, piece(k)],
            tok.at[2, piece(k)],
            tok_sem.at[1],
            across_recv.at[k],
            {"head": across},
        )

    def token_relay(k):
        return remote(
            tok.at[2, piece(k)],
            tok.at[3, piece(k)],
            tok_sem.at[1],
            diag_recv.at[k],
            {"head": pair},
        )

    for k in range(min(FLYING, pieces)):
        token_copy(k).start()
    pair_tokens = remote(tok.at[0], tok.at[1], tok_sem.at[1], tok_sem.at[2], {"head": pair})
    pair_tokens.start()
    for slot in range(EARLY_SLOTS, n_head):
        fetch(slot)

    def fetch_output_weights(k):
        count = heads // pieces
        at = pl.ds(k * count, count)
        for slot, owner in enumerate((h, across)):
            pltpu.make_async_copy(
                wo_hbm.at[at, block(owner, depth)], wo.at[0, slot, at], wo_sem.at[0]
            ).start()
        for slot, owner in enumerate((pair, diag)):
            remote(
                wo_hbm.at[at, block(owner, depth)],
                wo.at[1, slot, at],
                wo_sem.at[1],
                wo_sem.at[2],
                {"head": pair},
            ).start()

    def kv_copy(which, k, send, recv, target):
        at = kv[owners[k]].at[which, pl.ds(offsets[k], lengths[k])]
        return remote(at, at, send, recv, {"ctx": target})

    def sends(kind, index):
        return kv_send if early else kv_send.at[kind, index]

    def others(where, g):
        return other_recv.at[g] if early else other_recv.at[where, g]

    def direct_copy(shift, k):
        return kv_copy(c, k, sends(0, shift), same_recv.at[place, k], c + 2 * shift)

    def cross_copy(shift, k):
        target = ctx_pair + 2 * shift
        return kv_copy(c, k, sends(0, shift), others(place, owners[k]), target)

    def pair_copy(where, k):
        recv = others(where, owners[k])
        return kv_copy(2 * where + side, k, sends(1, where), recv, ctx_pair)

    def same_arrived(where, k):
        at = kv[owners[k]].at[2 * where + side, pl.ds(offsets[k], lengths[k])]
        came(at, same_recv.at[where, k])

    def relayed(k):
        if k in crossing:
            return 0
        return jnp.where(at_end, place - 1, place) if early else place

    def relay(k):
        def one(where, carry):
            same_arrived(where, k)
            pair_copy(where, k).start()
            return carry

        with scope(f"relay{k}"):
            lax.fori_loop(0, relayed(k), one, 0)

    def arrive(g):
        def other(where, carry):
            came(kv[g].at[2 * where + 1 - side], others(where, g))
            return carry

        def all_others(before):
            came(kv[g].at[pl.ds(0, before + 1)], other_recv.at[g])

        with scope(f"arrive{g}"):
            for k in range(pieces):
                if owners[k] == g:

                    def same(where, carry, k=k):
                        same_arrived(where, k)
                        return carry

                    lax.fori_loop(relayed(k), place, same, 0)
            if early:
                at_place(all_others)
            else:
                lax.fori_loop(0, place + 1, other, 0)

    shared, queries_at = pl.ds(0, 2 * size), pl.ds(2 * size, heads)

    def term(slot, at, wanted):
        return jnp.dot(
            tok[slot, at, :], weights[slot, :, wanted], preferred_element_type=f32
        )

    def begin():
        loaded(0)
        partial[...] = term(0, every, every)
        pair_tokens.wait_recv()
        loaded(1)
        partial[...] += term(1, every, every)
        loaded(2)
        loaded(3)

    def add_across(k):
        with scope(f"across{k}"):
            token_copy(k).wait_recv()
        token_relay(k).start()
        if k + FLYING < pieces:
            token_copy(k + FLYING).start()
        fetch_output_weights(k)
        return partial[piece(k), shared] + term(2, piece(k), shared)

    def finish_keys(k, found):
        with scope(f"diag{k}"):
            token_relay(k).wait_recv()
        found = found + term(3, piece(k), shared)
        kv[owners[k]][c, pl.ds(offsets[k], lengths[k]), :] = found.astype(bf16)

        def send(index, carry):
            direct_copy(later - index, k).start()
            if k in crossing:
                cross_copy(later - index, k).start()
            return carry

        lax.fori_loop(0, later, send, 0)
        if early and k not in crossing:

            @pl.when(later == 1)
            def _():
                cross_copy(1, k).start()

        pair_copy(place, k).start()

    def finish_queries():
        found = partial[:, queries_at]
        for slot in (2, 3):
            found = found + term(slot, every, queries_at)
        for g in range(group):
            query[g] = found[:, g * size : (g + 1) * size].astype(bf16)

    with scope("begin"):
        begin()
    for k in range(pieces):
        finish_keys(k, add_across(k))
        if k >= LAG:
            relay(k - LAG)
    with scope("queries"):
        finish_queries()
    waiting = list(range(max(pieces - LAG, 0), pieces))

    factor = (size ** (-0.5)) * math.log2(math.e)

    def fold(values, op):
        result = values[:, :LANES]
        for index in range(1, values.shape[1] // LANES):
            result = op(result, values[:, index * LANES : (index + 1) * LANES])
        return result

    def queries_of(at, count):
        return query[:, at, :].reshape(group * count, size)

    def product(queries, keys):
        return lax.dot_general(
            queries, keys, (((1,), (1,)), ((), ())), preferred_element_type=f32
        )

    def mask(found, low, count, g):
        width = found.shape[1]
        column = lax.broadcasted_iota(jnp.int32, (count, width), 1)
        shift = sizes[g].bit_length() - 1
        at_key = (column >> shift) * rows + (column & (sizes[g] - 1)) + first_row[g]
        at_query = lax.broadcasted_iota(jnp.int32, (count, width), 0) + low
        allowed = at_key <= at_query + side * rows
        return jnp.where(jnp.concatenate([allowed] * group, axis=0), found, NEG_LARGE)

    def keys_of(g, where, places):
        return kv[g][pl.ds(2 * where, 2 * places), :, pl.ds(0, size)].reshape(-1, size)

    def values_of(g, where, places):
        return kv[g][pl.ds(2 * where, 2 * places), :, pl.ds(size, size)].reshape(-1, size)

    def score(at, low, count, g, before):
        found = product(queries_of(at, count), keys_of(g, 0, before + 1))
        split = 2 * before * sizes[g]
        tail = mask(found[:, split:], low, count, g)
        scores[g][:, at, pl.ds(split, 2 * sizes[g])] = tail.reshape(group, count, -1)
        top = fold(tail, jnp.maximum)
        if split:
            head = found[:, :split]
            scores[g][:, at, pl.ds(0, split)] = head.reshape(group, count, split)
            top = jnp.maximum(top, fold(head, jnp.maximum))
        return top

    def weigh(found, top, values, state):
        total, summed = state
        weighed = jnp.exp2((found - top) * factor)
        summed = summed + jnp.dot(weighed.astype(bf16), values, preferred_element_type=f32)
        return total + fold(weighed, jnp.add), summed

    def close(at, count, state):
        total, summed = state
        total = jnp.sum(total, axis=-1, keepdims=True)
        mixed = (summed / total).astype(bf16)
        for g in range(group):
            att_own[at, pl.ds(g * size, size)] = mixed[g * count : (g + 1) * count]

    def nothing(count):
        return tuple(jnp.zeros((group * count, width), f32) for width in (LANES, size))

    def attention(at, low, count, before):
        top = top_ref[:, at, :].reshape(group * count, LANES)
        top = jnp.maximum(top, score(at, low, count, groups - 1, before))
        top = jnp.max(top, axis=-1, keepdims=True)
        state = nothing(count)
        for g in range(groups):
            width = 2 * (before + 1) * sizes[g]
            found = scores[g][:, at, pl.ds(0, width)].reshape(group * count, width)
            state = weigh(found, top, values_of(g, 0, before + 1), state)
        close(at, count, state)

    def attention_at_length(at, low, count):
        queries = queries_of(at, count)
        here = pl.ds(0, group * count)
        top = jnp.full((group * count, LANES), NEG_LARGE, f32)
        for g in range(groups):

            def first_pass(where, top, g=g):
                found = product(queries, keys_of(g, where, 1))
                scores[g][where, here] = found
                return jnp.maximum(top, fold(found, jnp.maximum))

            found = mask(product(queries, keys_of(g, place, 1)), low, count, g)
            scores[g][place, here] = found
            top = jnp.maximum(top, fold(found, jnp.maximum))
            top = lax.fori_loop(0, place, first_pass, top)
        top = jnp.max(top, axis=-1, keepdims=True)
        state = nothing(count)
        for g in range(groups):

            def second_pass(where, state, g=g):
                return weigh(scores[g][where, here], top, values_of(g, where, 1), state)

            state = lax.fori_loop(0, place + 1, second_pass, state)
        close(at, count, state)

    def prepare(g):
        count = min(2 * STEP, rows)

        def run(before):
            def one(index, carry):
                at = block(index, count)
                top = score(at, index * count, count, g, before)
                top = top.reshape(group, count, LANES)
                if g > 0:
                    top = jnp.maximum(top, top_ref[:, at, :])
                top_ref[:, at, :] = top
                return carry

            lax.fori_loop(0, rows // count, one, 0)

        with scope(f"prepare{g}"):
            at_place(run)

    for k in waiting[:-2]:
        relay(k)
    if early:
        arrive(0)
        prepare(0)
        for k in waiting[-2:]:
            relay(k)
        for g in range(1, groups - 1):
            arrive(g)
            prepare(g)
        arrive(groups - 1)
    else:
        for k in waiting[-2:]:
            relay(k)
        for g in range(groups):
            arrive(g)

    with scope("wo"):
        pltpu.make_async_copy(wo.at[0], wo.at[0], wo_sem.at[0]).wait()
        came(wo.at[1], wo_sem.at[2])

    chunks = [(0, STEP // 2), (STEP // 2, STEP // 2)]
    chunks += [(low, STEP) for low in range(STEP, rows, STEP)]

    def att_copy(k, at):
        return remote(
            att_own.at[at], att_pair.at[at], a_send, a_recv.at[k], {"head": pair}
        )

    def far_copy(k, at):
        return remote(
            far_send.at[at],
            far_part.at[at],
            tok_sem.at[1],
            r_recv.at[k],
            {"head": across},
        )

    def attend(k, at, low, count):
        with scope("attention"):
            if early:
                at_place(functools.partial(attention, at, low, count))
            else:
                attention_at_length(at, low, count)
        att_copy(k, at).start()

    def mix(ref, at, source, slot):
        return jnp.dot(ref[at, :], wo[source, slot], preferred_element_type=f32)

    def share(k, at):
        own = mix(att_own, at, 0, 1)
        with scope("exchange"):
            att_copy(k, at).wait_recv()
        with scope("mix"):
            far_send[at, :] = (own + mix(att_pair, at, 1, 1)).astype(bf16)
            far_copy(k, at).start()

    def static(k):
        low, count = chunks[k]
        return pl.ds(low, count), low, count

    attend(0, *static(0))
    attend(1, *static(1))
    share(0, static(0)[0])
    full = rows // STEP

    def attend_full(index):
        attend(index + 1, block(index, STEP), index * STEP, STEP)

    if full > 1:
        attend_full(1)
    share(1, static(1)[0])

    def both(index, carry):
        attend_full(index + 1)
        share(index + 1, block(index, STEP))
        return carry

    lax.fori_loop(1, full - 1, both, 0)
    if full > 1:
        share(full, block(full - 1, STEP))
    with scope("keep"):
        own_sum[...] = mix(att_own, every, 0, 0) + mix(att_pair, every, 1, 0)

    for k, (low, count) in enumerate(chunks):
        at = pl.ds(low, count)
        with scope(f"far{k}"):
            far_copy(k, at).wait_recv()
        out[at, :] = (own_sum[at, :] + far_part[at, :].astype(f32)).astype(out.dtype)

    with scope("sent"):
        sent(tok, tok_sem.at[1])
        sent(wo.at[1], wo_sem.at[1])
        sent(att_own, a_send)
        crossed = sum(lengths[k] for k in crossing)
        straight = rows - crossed

        def keys_sent(before):
            ahead = columns - 1 - before
            count = rows + ahead * (rows + crossed)
            count += straight * ((before if ahead else before - 1) + (ahead == 1))
            sent(weights.at[pl.ds(0, 2), pl.ds(0, count // 2), shared], kv_send)

        def direct_sent(shift, carry):
            sent(partial_keys, sends(0, shift))
            return carry

        def pair_sent(where, carry):
            sent(partial_keys, sends(1, where))
            return carry

        if early:
            at_place(keys_sent)
        else:
            partial_keys = far_send.at[:, shared]
            lax.fori_loop(1, later + 1, direct_sent, 0)
            lax.fori_loop(0, place + 1, pair_sent, 0)


def solution(mesh):
    n_ctx, n_head = mesh.shape["ctx"], mesh.shape["head"]

    def local(tokens, w_query, key_matrix, value_matrix, w_output):
        rows, depth = tokens.shape
        size = key_matrix.shape[1]
        heads = w_query.shape[1]
        group = heads // size
        columns = n_ctx // 2
        early = columns <= UNROLLED
        shares = SHORT_GROUPS if early else LONG_GROUPS
        unit = rows // sum(sum(share) for share in shares)
        sizes = [sum(share) * unit for share in shares]
        pieces = sum(len(share) for share in shares)
        groups = len(shares)
        chunks = rows // STEP + 1
        bf16, f32 = jnp.bfloat16, jnp.float32
        dma = pltpu.SemaphoreType.DMA
        vmem = pltpu.VMEM

        def found(length):
            if early:
                return vmem((group, rows, n_ctx * length), f32)
            return vmem((columns, group * STEP, 2 * length), f32)

        return pl.pallas_call(
            functools.partial(layer_kernel, n_ctx, n_head, shares, early),
            out_shape=vmem((rows, depth), bf16),
            in_specs=[pl.BlockSpec(memory_space=pltpu.HBM)] * 5,
            out_specs=pl.BlockSpec(memory_space=pltpu.VMEM),
            scratch_shapes=[
                vmem((n_head, depth, 2 * size + heads), bf16),
                vmem((2, 2, heads, depth), bf16),
                vmem((n_head, rows, depth), bf16),
                vmem((rows, 2 * size + heads), f32),
                vmem((group, rows, size), bf16),
                vmem((group, rows, LANES), f32),
                vmem((rows, heads), bf16),
                vmem((rows, heads), bf16),
                vmem((rows, depth), f32),
                vmem((rows, depth), bf16),
                vmem((rows, depth), bf16),
                *[vmem((n_ctx, length, 2 * size), bf16) for length in sizes],
                *[found(length) for length in sizes],
                dma((n_head,)),
                dma((3,)),
                dma((3,)),
                dma((pieces,)),
                dma((pieces,)),
                dma if early else dma((2, columns)),
                dma((columns - 1, pieces)),
                dma((groups,)) if early else dma((columns, groups)),
                dma,
                dma((chunks,)),
                dma((chunks,)),
            ],
            compiler_params=pltpu.CompilerParams(
                collective_id=0,
                has_side_effects=True,
                vmem_limit_bytes=63 * 1024 * 1024,
            ),
        )(tokens, w_query, key_matrix, value_matrix, w_output)

    return jax.shard_map(
        local,
        mesh=mesh,
        in_specs=(
            P("ctx", "head"),
            P(None, "head"),
            P(None, "head"),
            P(None, "head"),
            P("head", None),
        ),
        out_specs=P("ctx", "head"),
        check_vma=False,
    )
```

```python
import functools
import math

import jax
import jax.numpy as jnp
from jax import lax
from jax.experimental import pallas as pl
from jax.experimental.pallas import tpu as pltpu
from jax.sharding import PartitionSpec as P

MESH = pl.DeviceIdType.MESH
SHORT_GROUPS = ((1, 1, 1, 1), (1, 1), (1, 1))
LONG_GROUPS = ((2,), (2,), (2,), (2,))
CROSSING = (7,)
FLYING = 4
LAG = 2
SHORTCUT = (0, 1, 2, 3, 4, 5, 6)
NEAREST = True
EARLY_SLOTS = 2
STEP = 64
LANES = 128
UNROLLED = 4
NEG_LARGE = -1e30

scope = jax.named_scope


def layer_kernel(n_ctx, n_head, shares, early, *refs):
    groups = len(shares)
    tokens, wq_hbm, wk_hbm, wv_hbm, wo_hbm, out = refs[:6]
    weights, wo, tok, partial, query, top_ref, att_own, att_pair = refs[6:14]
    own_sum, far_send, far_part = refs[14:17]
    kv = refs[17 : 17 + groups]
    scores = refs[17 + groups : 17 + 2 * groups]
    (
        w_sem,
        wo_sem,
        tok_sem,
        across_recv,
        diag_recv,
        kv_send,
        same_recv,
        other_recv,
        a_send,
        a_recv,
        r_recv,
        ready,
    ) = refs[17 + 2 * groups :]
    rows, depth = tokens.shape
    size = wk_hbm.shape[1]
    heads = wq_hbm.shape[1]
    group = heads // size
    c = lax.axis_index("ctx")
    h = lax.axis_index("head")
    place, side = c // 2, c % 2
    core = h % 2
    pair = h + 1 - 2 * core
    across = (h + 2) % n_head
    diag = across + 1 - 2 * core
    ctx_pair = c + 1 - 2 * side
    columns = n_ctx // 2
    later = columns - 1 - place
    at_end = later == 0
    f32, bf16 = jnp.float32, jnp.bfloat16
    every = slice(None)

    unit = rows // sum(sum(share) for share in shares)
    lengths, starts, owners, offsets, first_row = [], [], [], [], []
    row = 0
    for g, share in enumerate(shares):
        first_row.append(row)
        for count in share:
            owners.append(g)
            starts.append(row)
            offsets.append(row - first_row[g])
            lengths.append(count * unit)
            row += count * unit
    pieces = len(lengths)
    sizes = [sum(share) * unit for share in shares]
    last = pieces - 1
    crossing = CROSSING if early else ()
    shortcut = SHORTCUT if early else ()

    def remote(src, dst, send, recv, target):
        return pltpu.make_async_remote_copy(
            src_ref=src,
            dst_ref=dst,
            send_sem=send,
            recv_sem=recv,
            device_id=target,
            device_id_type=MESH,
        )

    def sent(ref, sem):
        remote(ref, ref, sem, sem, {"head": pair}).wait_send()

    def came(ref, sem):
        remote(ref, ref, sem, sem, {"head": pair}).wait_recv()

    def at_place(call):
        for before in range(columns):
            pl.when(place == before)(functools.partial(call, before))

    def block(index, count):
        return pl.ds(pl.multiple_of(index * count, count), count)

    def piece(k):
        return pl.ds(starts[k], lengths[k])

    own_load = pltpu.make_async_copy(tokens, tok.at[0], tok_sem.at[0])
    own_load.start()
    barrier = pltpu.get_barrier_semaphore()

    def greet(target):
        pl.semaphore_signal(barrier, inc=1, device_id=target, device_id_type=MESH)

    per_place = 2 if early else 1

    def greet_later(shift, carry):
        greet({"ctx": c + 2 * shift})
        if early:
            greet({"ctx": ctx_pair + 2 * shift})
        return carry

    def answer(where, carry):
        for which in (side, 1 - side)[:per_place]:
            pl.semaphore_signal(
                ready, inc=1, device_id={"ctx": 2 * where + which}, device_id_type=MESH
            )
        return carry

    greet({"head": pair})
    greet({"head": across})
    greet({"ctx": ctx_pair})
    lax.fori_loop(1, later + 1, greet_later, 0)
    with scope("own"):
        own_load.wait()
    def fetch(slot):
        at = block((h, pair, across, diag)[slot], depth)
        into = weights.at[slot]
        for src, low, width in (
            (wk_hbm, 0, size),
            (wv_hbm, size, size),
            (wq_hbm, 2 * size, heads),
        ):
            pltpu.make_async_copy(
                src.at[at], into.at[:, pl.ds(low, width)], w_sem.at[slot]
            ).start()

    def loaded(slot):
        pltpu.make_async_copy(weights.at[slot], weights.at[slot], w_sem.at[slot]).wait()

    for slot in range(EARLY_SLOTS):
        fetch(slot)
    with scope("barrier"):
        pl.semaphore_wait(barrier, 3 + per_place * place)

    def token_copy(k):
        return remote(
            tok.at[0, piece(k)],
            tok.at[2, piece(k)],
            tok_sem.at[1],
            across_recv.at[k],
            {"head": across},
        )

    def token_relay(k):
        return remote(
            tok.at[2, piece(k)],
            tok.at[3, piece(k)],
            tok_sem.at[1],
            diag_recv.at[k],
            {"head": pair},
        )

    for k in range(min(FLYING, pieces)):
        token_copy(k).start()
    pair_tokens = remote(tok.at[0], tok.at[1], tok_sem.at[1], tok_sem.at[2], {"head": pair})
    pair_tokens.start()
    lax.fori_loop(0, place, answer, 0)
    for slot in range(EARLY_SLOTS, n_head):
        fetch(slot)

    def fetch_output_weights(k):
        count = heads // pieces
        at = pl.ds(k * count, count)
        for slot, owner in enumerate((h, across)):
            pltpu.make_async_copy(
                wo_hbm.at[at, block(owner, depth)], wo.at[0, slot, at], wo_sem.at[0]
            ).start()
        for slot, owner in enumerate((pair, diag)):
            remote(
                wo_hbm.at[at, block(owner, depth)],
                wo.at[1, slot, at],
                wo_sem.at[1],
                wo_sem.at[2],
                {"head": pair},
            ).start()

    def kv_copy(which, k, send, recv, target):
        at = kv[owners[k]].at[which, pl.ds(offsets[k], lengths[k])]
        return remote(at, at, send, recv, {"ctx": target})

    def sends(kind, index):
        return kv_send if early else kv_send.at[kind, index]

    def others(where, g):
        return other_recv.at[g] if early else other_recv.at[where, g]

    def direct_copy(shift, k):
        return kv_copy(c, k, sends(0, shift), same_recv.at[place, k], c + 2 * shift)

    def cross_copy(shift, k):
        target = ctx_pair + 2 * shift
        return kv_copy(c, k, sends(0, shift), others(place, owners[k]), target)

    def pair_copy(where, k):
        recv = others(where, owners[k])
        return kv_copy(2 * where + side, k, sends(1, where), recv, ctx_pair)

    def same_arrived(where, k):
        at = kv[owners[k]].at[2 * where + side, pl.ds(offsets[k], lengths[k])]
        came(at, same_recv.at[where, k])

    def relayed(k):
        if k in crossing:
            return 0
        return jnp.where(at_end, place - 1, place) if k in shortcut else place

    def relay(k):
        def one(where, carry):
            same_arrived(where, k)
            pair_copy(where, k).start()
            return carry

        with scope(f"relay{k}"):
            lax.fori_loop(0, relayed(k), one, 0)

    def arrive(g):
        def other(where, carry):
            came(kv[g].at[2 * where + 1 - side], others(where, g))
            return carry

        def all_others(before):
            came(kv[g].at[pl.ds(0, before + 1)], other_recv.at[g])

        with scope(f"arrive{g}"):
            for k in range(pieces):
                if owners[k] == g:

                    def same(where, carry, k=k):
                        same_arrived(where, k)
                        return carry

                    lax.fori_loop(relayed(k), place, same, 0)
            if early:
                at_place(all_others)
            else:
                lax.fori_loop(0, place + 1, other, 0)

    shared, queries_at = pl.ds(0, 2 * size), pl.ds(2 * size, heads)

    def term(slot, at, wanted):
        return jnp.dot(
            tok[slot, at, :], weights[slot, :, wanted], preferred_element_type=f32
        )

    def begin():
        loaded(0)
        partial[...] = term(0, every, every)
        pair_tokens.wait_recv()
        loaded(1)
        partial[...] += term(1, every, every)
        loaded(2)
        loaded(3)

    def add_across(k):
        with scope(f"across{k}"):
            token_copy(k).wait_recv()
        token_relay(k).start()
        if k + FLYING < pieces:
            token_copy(k + FLYING).start()
        fetch_output_weights(k)
        return partial[piece(k), shared] + term(2, piece(k), shared)

    def finish_keys(k, found):
        with scope(f"diag{k}"):
            token_relay(k).wait_recv()
        found = found + term(3, piece(k), shared)
        kv[owners[k]][c, pl.ds(offsets[k], lengths[k]), :] = found.astype(bf16)

        def send(index, carry):
            shift = index + 1 if NEAREST else later - index
            direct_copy(shift, k).start()
            if k in crossing:
                cross_copy(shift, k).start()
            return carry

        if k == 0:

            @pl.when(later > 0)
            def _():
                pl.semaphore_wait(ready, per_place * later)

        lax.fori_loop(0, later, send, 0)
        if k in shortcut:

            @pl.when(later == 1)
            def _():
                cross_copy(1, k).start()

        pair_copy(place, k).start()

    def finish_queries():
        found = partial[:, queries_at]
        for slot in (2, 3):
            found = found + term(slot, every, queries_at)
        for g in range(group):
            query[g] = found[:, g * size : (g + 1) * size].astype(bf16)

    with scope("begin"):
        begin()
    for k in range(pieces):
        finish_keys(k, add_across(k))
        if k >= LAG:
            relay(k - LAG)
    with scope("queries"):
        finish_queries()
    waiting = list(range(max(pieces - LAG, 0), pieces))

    factor = (size ** (-0.5)) * math.log2(math.e)

    def fold(values, op):
        result = values[:, :LANES]
        for index in range(1, values.shape[1] // LANES):
            result = op(result, values[:, index * LANES : (index + 1) * LANES])
        return result

    def queries_of(at, count):
        return query[:, at, :].reshape(group * count, size)

    def product(queries, keys):
        return lax.dot_general(
            queries, keys, (((1,), (1,)), ((), ())), preferred_element_type=f32
        )

    def mask(found, low, count, g):
        width = found.shape[1]
        column = lax.broadcasted_iota(jnp.int32, (count, width), 1)
        shift = sizes[g].bit_length() - 1
        at_key = (column >> shift) * rows + (column & (sizes[g] - 1)) + first_row[g]
        at_query = lax.broadcasted_iota(jnp.int32, (count, width), 0) + low
        allowed = at_key <= at_query + side * rows
        return jnp.where(jnp.concatenate([allowed] * group, axis=0), found, NEG_LARGE)

    def keys_of(g, where, places):
        return kv[g][pl.ds(2 * where, 2 * places), :, pl.ds(0, size)].reshape(-1, size)

    def values_of(g, where, places):
        return kv[g][pl.ds(2 * where, 2 * places), :, pl.ds(size, size)].reshape(-1, size)

    def score(at, low, count, g, before):
        found = product(queries_of(at, count), keys_of(g, 0, before + 1))
        split = 2 * before * sizes[g]
        tail = mask(found[:, split:], low, count, g)
        scores[g][:, at, pl.ds(split, 2 * sizes[g])] = tail.reshape(group, count, -1)
        top = fold(tail, jnp.maximum)
        if split:
            head = found[:, :split]
            scores[g][:, at, pl.ds(0, split)] = head.reshape(group, count, split)
            top = jnp.maximum(top, fold(head, jnp.maximum))
        return top

    def weigh(found, top, values, state):
        total, summed = state
        weighed = jnp.exp2((found - top) * factor)
        summed = summed + jnp.dot(weighed.astype(bf16), values, preferred_element_type=f32)
        return total + fold(weighed, jnp.add), summed

    def close(at, count, state):
        total, summed = state
        total = jnp.sum(total, axis=-1, keepdims=True)
        mixed = (summed / total).astype(bf16)
        for g in range(group):
            att_own[at, pl.ds(g * size, size)] = mixed[g * count : (g + 1) * count]

    def nothing(count):
        return tuple(jnp.zeros((group * count, width), f32) for width in (LANES, size))

    def attention(at, low, count, before):
        top = top_ref[:, at, :].reshape(group * count, LANES)
        top = jnp.maximum(top, score(at, low, count, groups - 1, before))
        top = jnp.max(top, axis=-1, keepdims=True)
        state = nothing(count)
        for g in range(groups):
            width = 2 * (before + 1) * sizes[g]
            found = scores[g][:, at, pl.ds(0, width)].reshape(group * count, width)
            state = weigh(found, top, values_of(g, 0, before + 1), state)
        close(at, count, state)

    def attention_at_length(at, low, count):
        queries = queries_of(at, count)
        here = pl.ds(0, group * count)
        top = jnp.full((group * count, LANES), NEG_LARGE, f32)
        for g in range(groups):

            def first_pass(where, top, g=g):
                found = product(queries, keys_of(g, where, 1))
                scores[g][where, here] = found
                return jnp.maximum(top, fold(found, jnp.maximum))

            found = mask(product(queries, keys_of(g, place, 1)), low, count, g)
            scores[g][place, here] = found
            top = jnp.maximum(top, fold(found, jnp.maximum))
            top = lax.fori_loop(0, place, first_pass, top)
        top = jnp.max(top, axis=-1, keepdims=True)
        state = nothing(count)
        for g in range(groups):

            def second_pass(where, state, g=g):
                return weigh(scores[g][where, here], top, values_of(g, where, 1), state)

            state = lax.fori_loop(0, place + 1, second_pass, state)
        close(at, count, state)

    def prepare(g):
        count = min(2 * STEP, rows)

        def run(before):
            def one(index, carry):
                at = block(index, count)
                top = score(at, index * count, count, g, before)
                top = top.reshape(group, count, LANES)
                if g > 0:
                    top = jnp.maximum(top, top_ref[:, at, :])
                top_ref[:, at, :] = top
                return carry

            lax.fori_loop(0, rows // count, one, 0)

        with scope(f"prepare{g}"):
            at_place(run)

    for k in waiting:
        relay(k)
    if early:
        arrive(0)
        prepare(0)
        for g in range(1, groups - 1):
            arrive(g)
            prepare(g)
        arrive(groups - 1)
    else:
        for g in range(groups):
            arrive(g)

    with scope("wo"):
        pltpu.make_async_copy(wo.at[0], wo.at[0], wo_sem.at[0]).wait()
        came(wo.at[1], wo_sem.at[2])

    chunks = [(0, STEP // 2), (STEP // 2, STEP // 2)]
    chunks += [(low, STEP) for low in range(STEP, rows, STEP)]

    def att_copy(k, at):
        return remote(
            att_own.at[at], att_pair.at[at], a_send, a_recv.at[k], {"head": pair}
        )

    def far_copy(k, at):
        return remote(
            far_send.at[at],
            far_part.at[at],
            tok_sem.at[1],
            r_recv.at[k],
            {"head": across},
        )

    def attend(k, at, low, count):
        with scope("attention"):
            if early:
                at_place(functools.partial(attention, at, low, count))
            else:
                attention_at_length(at, low, count)
        att_copy(k, at).start()

    def mix(ref, at, source, slot):
        return jnp.dot(ref[at, :], wo[source, slot], preferred_element_type=f32)

    def share(k, at):
        own = mix(att_own, at, 0, 1)
        with scope("exchange"):
            att_copy(k, at).wait_recv()
        with scope("mix"):
            far_send[at, :] = (own + mix(att_pair, at, 1, 1)).astype(bf16)
            far_copy(k, at).start()

    def static(k):
        low, count = chunks[k]
        return pl.ds(low, count), low, count

    attend(0, *static(0))
    attend(1, *static(1))
    share(0, static(0)[0])
    full = rows // STEP

    def attend_full(index):
        attend(index + 1, block(index, STEP), index * STEP, STEP)

    if full > 1:
        attend_full(1)
    share(1, static(1)[0])

    def both(index, carry):
        attend_full(index + 1)
        share(index + 1, block(index, STEP))
        return carry

    lax.fori_loop(1, full - 1, both, 0)
    if full > 1:
        share(full, block(full - 1, STEP))
    with scope("keep"):
        own_sum[...] = mix(att_own, every, 0, 0) + mix(att_pair, every, 1, 0)

    for k, (low, count) in enumerate(chunks):
        at = pl.ds(low, count)
        with scope(f"far{k}"):
            far_copy(k, at).wait_recv()
        out[at, :] = (own_sum[at, :] + far_part[at, :].astype(f32)).astype(out.dtype)

    with scope("sent"):
        sent(tok, tok_sem.at[1])
        sent(wo.at[1], wo_sem.at[1])
        sent(att_own, a_send)
        crossed = sum(lengths[k] for k in crossing)
        straight = rows - crossed
        short = sum(lengths[k] for k in shortcut)

        def keys_sent(before):
            ahead = columns - 1 - before
            count = rows + ahead * (rows + crossed)
            count += straight * before
            if ahead == 0:
                count -= short
            if ahead == 1:
                count += short
            sent(weights.at[pl.ds(0, 2), pl.ds(0, count // 2), shared], kv_send)

        def direct_sent(shift, carry):
            sent(partial_keys, sends(0, shift))
            return carry

        def pair_sent(where, carry):
            sent(partial_keys, sends(1, where))
            return carry

        if early:
            at_place(keys_sent)
        else:
            partial_keys = far_send.at[:, shared]
            lax.fori_loop(1, later + 1, direct_sent, 0)
            lax.fori_loop(0, place + 1, pair_sent, 0)


def solution(mesh):
    n_ctx, n_head = mesh.shape["ctx"], mesh.shape["head"]

    def local(tokens, w_query, key_matrix, value_matrix, w_output):
        rows, depth = tokens.shape
        size = key_matrix.shape[1]
        heads = w_query.shape[1]
        group = heads // size
        columns = n_ctx // 2
        early = columns <= UNROLLED
        shares = SHORT_GROUPS if early else LONG_GROUPS
        unit = rows // sum(sum(share) for share in shares)
        sizes = [sum(share) * unit for share in shares]
        pieces = sum(len(share) for share in shares)
        groups = len(shares)
        chunks = rows // STEP + 1
        bf16, f32 = jnp.bfloat16, jnp.float32
        dma = pltpu.SemaphoreType.DMA
        vmem = pltpu.VMEM

        def found(length):
            if early:
                return vmem((group, rows, n_ctx * length), f32)
            return vmem((columns, group * STEP, 2 * length), f32)

        return pl.pallas_call(
            functools.partial(layer_kernel, n_ctx, n_head, shares, early),
            out_shape=vmem((rows, depth), bf16),
            in_specs=[pl.BlockSpec(memory_space=pltpu.HBM)] * 5,
            out_specs=pl.BlockSpec(memory_space=pltpu.VMEM),
            scratch_shapes=[
                vmem((n_head, depth, 2 * size + heads), bf16),
                vmem((2, 2, heads, depth), bf16),
                vmem((n_head, rows, depth), bf16),
                vmem((rows, 2 * size + heads), f32),
                vmem((group, rows, size), bf16),
                vmem((group, rows, LANES), f32),
                vmem((rows, heads), bf16),
                vmem((rows, heads), bf16),
                vmem((rows, depth), f32),
                vmem((rows, depth), bf16),
                vmem((rows, depth), bf16),
                *[vmem((n_ctx, length, 2 * size), bf16) for length in sizes],
                *[found(length) for length in sizes],
                dma((n_head,)),
                dma((3,)),
                dma((3,)),
                dma((pieces,)),
                dma((pieces,)),
                dma if early else dma((2, columns)),
                dma((columns - 1, pieces)),
                dma((groups,)) if early else dma((columns, groups)),
                dma,
                dma((chunks,)),
                dma((chunks,)),
                pltpu.SemaphoreType.REGULAR,
            ],
            compiler_params=pltpu.CompilerParams(
                collective_id=0,
                has_side_effects=True,
                vmem_limit_bytes=63 * 1024 * 1024,
            ),
        )(tokens, w_query, key_matrix, value_matrix, w_output)

    return jax.shard_map(
        local,
        mesh=mesh,
        in_specs=(
            P("ctx", "head"),
            P(None, "head"),
            P(None, "head"),
            P(None, "head"),
            P("head", None),
        ),
        out_specs=P("ctx", "head"),
        check_vma=False,
    )
```

```python
import functools
import math

import jax
import jax.numpy as jnp
from jax import lax
from jax.experimental import pallas as pl
from jax.experimental.pallas import tpu as pltpu
from jax.sharding import PartitionSpec as P

MESH = pl.DeviceIdType.MESH
SHORT_GROUPS = ((1, 1, 1, 1), (1, 1), (1, 1))
LONG_GROUPS = ((2,), (2,), (2,), (2,))
CROSSING = (7,)
FLYING = 4
LAG = 2
SHORTCUT = (0, 1, 2, 3, 4, 5, 6)
EARLY_SLOTS = 2
STEP = 64
LANES = 128
UNROLLED = 4
NEG_LARGE = -1e30

scope = jax.named_scope


def layer_kernel(n_ctx, n_head, shares, early, *refs):
    groups = len(shares)
    tokens, wq_hbm, wk_hbm, wv_hbm, wo_hbm, out = refs[:6]
    weights, wo, tok, partial, query, top_ref, att_own, att_pair = refs[6:14]
    own_sum, far_send, far_part = refs[14:17]
    kv = refs[17 : 17 + groups]
    scores = refs[17 + groups : 17 + 2 * groups]
    (
        w_sem,
        wo_sem,
        tok_sem,
        across_recv,
        diag_recv,
        kv_send,
        same_recv,
        other_recv,
        a_send,
        a_recv,
        r_recv,
        ready,
    ) = refs[17 + 2 * groups :]
    rows, depth = tokens.shape
    size = wk_hbm.shape[1]
    heads = wq_hbm.shape[1]
    group = heads // size
    c = lax.axis_index("ctx")
    h = lax.axis_index("head")
    place, side = c // 2, c % 2
    core = h % 2
    pair = h + 1 - 2 * core
    across = (h + 2) % n_head
    diag = across + 1 - 2 * core
    ctx_pair = c + 1 - 2 * side
    columns = n_ctx // 2
    later = columns - 1 - place
    at_end = later == 0
    f32, bf16 = jnp.float32, jnp.bfloat16
    every = slice(None)

    unit = rows // sum(sum(share) for share in shares)
    lengths, starts, owners, offsets, first_row = [], [], [], [], []
    row = 0
    for g, share in enumerate(shares):
        first_row.append(row)
        for count in share:
            owners.append(g)
            starts.append(row)
            offsets.append(row - first_row[g])
            lengths.append(count * unit)
            row += count * unit
    pieces = len(lengths)
    sizes = [sum(share) * unit for share in shares]
    last = pieces - 1
    crossing = CROSSING if early else ()
    shortcut = SHORTCUT if early else ()

    def remote(src, dst, send, recv, target):
        return pltpu.make_async_remote_copy(
            src_ref=src,
            dst_ref=dst,
            send_sem=send,
            recv_sem=recv,
            device_id=target,
            device_id_type=MESH,
        )

    def sent(ref, sem):
        remote(ref, ref, sem, sem, {"head": pair}).wait_send()

    def came(ref, sem):
        remote(ref, ref, sem, sem, {"head": pair}).wait_recv()

    def at_place(call):
        for before in range(columns):
            pl.when(place == before)(functools.partial(call, before))

    def block(index, count):
        return pl.ds(pl.multiple_of(index * count, count), count)

    def piece(k):
        return pl.ds(starts[k], lengths[k])

    own_load = pltpu.make_async_copy(tokens, tok.at[0], tok_sem.at[0])
    own_load.start()
    barrier = pltpu.get_barrier_semaphore()

    def greet(target):
        pl.semaphore_signal(barrier, inc=1, device_id=target, device_id_type=MESH)

    per_place = 2 if early else 1

    def greet_later(shift, carry):
        greet({"ctx": c + 2 * shift})
        if early:
            greet({"ctx": ctx_pair + 2 * shift})
        return carry

    def answer(where, carry):
        for which in (side, 1 - side)[:per_place]:
            pl.semaphore_signal(
                ready, inc=1, device_id={"ctx": 2 * where + which}, device_id_type=MESH
            )
        return carry

    greet({"head": pair})
    greet({"head": across})
    greet({"ctx": ctx_pair})
    lax.fori_loop(1, later + 1, greet_later, 0)
    with scope("own"):
        own_load.wait()
    def fetch(slot):
        at = block((h, pair, across, diag)[slot], depth)
        into = weights.at[slot]
        for src, low, width in (
            (wk_hbm, 0, size),
            (wv_hbm, size, size),
            (wq_hbm, 2 * size, heads),
        ):
            pltpu.make_async_copy(
                src.at[at], into.at[:, pl.ds(low, width)], w_sem.at[slot]
            ).start()

    def loaded(slot):
        pltpu.make_async_copy(weights.at[slot], weights.at[slot], w_sem.at[slot]).wait()

    for slot in range(EARLY_SLOTS):
        fetch(slot)
    with scope("barrier"):
        pl.semaphore_wait(barrier, 3 + per_place * place)

    def token_copy(k):
        return remote(
            tok.at[0, piece(k)],
            tok.at[2, piece(k)],
            tok_sem.at[1],
            across_recv.at[k],
            {"head": across},
        )

    def token_relay(k):
        return remote(
            tok.at[2, piece(k)],
            tok.at[3, piece(k)],
            tok_sem.at[1],
            diag_recv.at[k],
            {"head": pair},
        )

    for k in range(min(FLYING, pieces)):
        token_copy(k).start()
    pair_tokens = remote(tok.at[0], tok.at[1], tok_sem.at[1], tok_sem.at[2], {"head": pair})
    pair_tokens.start()
    lax.fori_loop(0, place, answer, 0)
    for slot in range(EARLY_SLOTS, n_head):
        fetch(slot)

    def fetch_output_weights(k):
        count = heads // pieces
        at = pl.ds(k * count, count)
        for slot, owner in enumerate((h, across)):
            pltpu.make_async_copy(
                wo_hbm.at[at, block(owner, depth)], wo.at[0, slot, at], wo_sem.at[0]
            ).start()
        for slot, owner in enumerate((pair, diag)):
            remote(
                wo_hbm.at[at, block(owner, depth)],
                wo.at[1, slot, at],
                wo_sem.at[1],
                wo_sem.at[2],
                {"head": pair},
            ).start()

    def kv_copy(which, k, send, recv, target):
        at = kv[owners[k]].at[which, pl.ds(offsets[k], lengths[k])]
        return remote(at, at, send, recv, {"ctx": target})

    def sends(kind, index):
        return kv_send if early else kv_send.at[kind, index]

    def others(where, g):
        return other_recv.at[g] if early else other_recv.at[where, g]

    def direct_copy(shift, k):
        return kv_copy(c, k, sends(0, shift), same_recv.at[place, k], c + 2 * shift)

    def cross_copy(shift, k):
        target = ctx_pair + 2 * shift
        return kv_copy(c, k, sends(0, shift), others(place, owners[k]), target)

    def pair_copy(where, k):
        recv = others(where, owners[k])
        return kv_copy(2 * where + side, k, sends(1, where), recv, ctx_pair)

    def same_arrived(where, k):
        at = kv[owners[k]].at[2 * where + side, pl.ds(offsets[k], lengths[k])]
        came(at, same_recv.at[where, k])

    def relayed(k):
        if k in crossing:
            return 0
        return jnp.where(at_end, place - 1, place) if k in shortcut else place

    def relay(k):
        def one(where, carry):
            same_arrived(where, k)
            pair_copy(where, k).start()
            return carry

        with scope(f"relay{k}"):
            lax.fori_loop(0, relayed(k), one, 0)

    def arrive(g):
        def other(where, carry):
            came(kv[g].at[2 * where + 1 - side], others(where, g))
            return carry

        def all_others(before):
            came(kv[g].at[pl.ds(0, before + 1)], other_recv.at[g])

        with scope(f"arrive{g}"):
            for k in range(pieces):
                if owners[k] == g:

                    def same(where, carry, k=k):
                        same_arrived(where, k)
                        return carry

                    lax.fori_loop(relayed(k), place, same, 0)
            if early:
                at_place(all_others)
            else:
                lax.fori_loop(0, place + 1, other, 0)

    shared, queries_at = pl.ds(0, 2 * size), pl.ds(2 * size, heads)

    def term(slot, at, wanted):
        return jnp.dot(
            tok[slot, at, :], weights[slot, :, wanted], preferred_element_type=f32
        )

    def begin():
        loaded(0)
        partial[...] = term(0, every, every)
        pair_tokens.wait_recv()
        loaded(1)
        partial[...] += term(1, every, every)
        loaded(2)
        loaded(3)

    def receive(k):
        with scope(f"across{k}"):
            token_copy(k).wait_recv()
        token_relay(k).start()
        if k + FLYING < pieces:
            token_copy(k + FLYING).start()
        fetch_output_weights(k)

    def finish_keys(k, found):
        with scope(f"diag{k}"):
            token_relay(k).wait_recv()
        found = found + term(3, piece(k), shared)
        kv[owners[k]][c, pl.ds(offsets[k], lengths[k]), :] = found.astype(bf16)

        def send(index, carry):
            shift = jnp.where(place == 0, index + 1, later - index)
            direct_copy(shift, k).start()
            if k in crossing:
                cross_copy(shift, k).start()
            return carry

        if k == 0:

            @pl.when(later > 0)
            def _():
                pl.semaphore_wait(ready, per_place * later)

        lax.fori_loop(0, later, send, 0)
        if k in shortcut:

            @pl.when(later == 1)
            def _():
                cross_copy(1, k).start()

        pair_copy(place, k).start()

    def finish_queries():
        found = partial[:, queries_at]
        for slot in (2, 3):
            found = found + term(slot, every, queries_at)
        for g in range(group):
            query[g] = found[:, g * size : (g + 1) * size].astype(bf16)

    with scope("begin"):
        begin()
    for k in range(pieces):
        if k == 0:
            receive(k)
        else:
            pl.when(core == 0)(functools.partial(receive, k))
        found = partial[piece(k), shared] + term(2, piece(k), shared)
        if k < last:
            pl.when(core == 1)(functools.partial(receive, k + 1))
        finish_keys(k, found)
        if k >= LAG:
            relay(k - LAG)
    with scope("queries"):
        finish_queries()
    waiting = list(range(max(pieces - LAG, 0), pieces))

    factor = (size ** (-0.5)) * math.log2(math.e)

    def fold(values, op):
        result = values[:, :LANES]
        for index in range(1, values.shape[1] // LANES):
            result = op(result, values[:, index * LANES : (index + 1) * LANES])
        return result

    def queries_of(at, count):
        return query[:, at, :].reshape(group * count, size)

    def product(queries, keys):
        return lax.dot_general(
            queries, keys, (((1,), (1,)), ((), ())), preferred_element_type=f32
        )

    def mask(found, low, count, g):
        width = found.shape[1]
        column = lax.broadcasted_iota(jnp.int32, (count, width), 1)
        shift = sizes[g].bit_length() - 1
        at_key = (column >> shift) * rows + (column & (sizes[g] - 1)) + first_row[g]
        at_query = lax.broadcasted_iota(jnp.int32, (count, width), 0) + low
        allowed = at_key <= at_query + side * rows
        return jnp.where(jnp.concatenate([allowed] * group, axis=0), found, NEG_LARGE)

    def keys_of(g, where, places):
        return kv[g][pl.ds(2 * where, 2 * places), :, pl.ds(0, size)].reshape(-1, size)

    def values_of(g, where, places):
        return kv[g][pl.ds(2 * where, 2 * places), :, pl.ds(size, size)].reshape(-1, size)

    def score(at, low, count, g, before):
        found = product(queries_of(at, count), keys_of(g, 0, before + 1))
        split = 2 * before * sizes[g]
        tail = mask(found[:, split:], low, count, g)
        scores[g][:, at, pl.ds(split, 2 * sizes[g])] = tail.reshape(group, count, -1)
        top = fold(tail, jnp.maximum)
        if split:
            head = found[:, :split]
            scores[g][:, at, pl.ds(0, split)] = head.reshape(group, count, split)
            top = jnp.maximum(top, fold(head, jnp.maximum))
        return top

    def weigh(found, top, values, state):
        total, summed = state
        weighed = jnp.exp2((found - top) * factor)
        summed = summed + jnp.dot(weighed.astype(bf16), values, preferred_element_type=f32)
        return total + fold(weighed, jnp.add), summed

    def close(at, count, state):
        total, summed = state
        total = jnp.sum(total, axis=-1, keepdims=True)
        mixed = (summed / total).astype(bf16)
        for g in range(group):
            att_own[at, pl.ds(g * size, size)] = mixed[g * count : (g + 1) * count]

    def nothing(count):
        return tuple(jnp.zeros((group * count, width), f32) for width in (LANES, size))

    def attention(at, low, count, before):
        top = top_ref[:, at, :].reshape(group * count, LANES)
        top = jnp.maximum(top, score(at, low, count, groups - 1, before))
        top = jnp.max(top, axis=-1, keepdims=True)
        state = nothing(count)
        for g in range(groups):
            width = 2 * (before + 1) * sizes[g]
            found = scores[g][:, at, pl.ds(0, width)].reshape(group * count, width)
            state = weigh(found, top, values_of(g, 0, before + 1), state)
        close(at, count, state)

    def attention_at_length(at, low, count):
        queries = queries_of(at, count)
        here = pl.ds(0, group * count)
        top = jnp.full((group * count, LANES), NEG_LARGE, f32)
        for g in range(groups):

            def first_pass(where, top, g=g):
                found = product(queries, keys_of(g, where, 1))
                scores[g][where, here] = found
                return jnp.maximum(top, fold(found, jnp.maximum))

            found = mask(product(queries, keys_of(g, place, 1)), low, count, g)
            scores[g][place, here] = found
            top = jnp.maximum(top, fold(found, jnp.maximum))
            top = lax.fori_loop(0, place, first_pass, top)
        top = jnp.max(top, axis=-1, keepdims=True)
        state = nothing(count)
        for g in range(groups):

            def second_pass(where, state, g=g):
                return weigh(scores[g][where, here], top, values_of(g, where, 1), state)

            state = lax.fori_loop(0, place + 1, second_pass, state)
        close(at, count, state)

    def prepare(g):
        count = min(2 * STEP, rows)

        def run(before):
            def one(index, carry):
                at = block(index, count)
                top = score(at, index * count, count, g, before)
                top = top.reshape(group, count, LANES)
                if g > 0:
                    top = jnp.maximum(top, top_ref[:, at, :])
                top_ref[:, at, :] = top
                return carry

            lax.fori_loop(0, rows // count, one, 0)

        with scope(f"prepare{g}"):
            at_place(run)

    for k in waiting:
        relay(k)
    if early:
        arrive(0)
        prepare(0)
        for g in range(1, groups - 1):
            arrive(g)
            prepare(g)
        arrive(groups - 1)
    else:
        for g in range(groups):
            arrive(g)

    with scope("wo"):
        pltpu.make_async_copy(wo.at[0], wo.at[0], wo_sem.at[0]).wait()
        came(wo.at[1], wo_sem.at[2])

    chunks = [(0, STEP // 2), (STEP // 2, STEP // 2)]
    chunks += [(low, STEP) for low in range(STEP, rows, STEP)]

    def att_copy(k, at):
        return remote(
            att_own.at[at], att_pair.at[at], a_send, a_recv.at[k], {"head": pair}
        )

    def far_copy(k, at):
        return remote(
            far_send.at[at],
            far_part.at[at],
            tok_sem.at[1],
            r_recv.at[k],
            {"head": across},
        )

    def attend(k, at, low, count):
        with scope("attention"):
            if early:
                at_place(functools.partial(attention, at, low, count))
            else:
                attention_at_length(at, low, count)
        att_copy(k, at).start()

    def mix(ref, at, source, slot):
        return jnp.dot(ref[at, :], wo[source, slot], preferred_element_type=f32)

    def share(k, at):
        own = mix(att_own, at, 0, 1)
        with scope("exchange"):
            att_copy(k, at).wait_recv()
        with scope("mix"):
            far_send[at, :] = (own + mix(att_pair, at, 1, 1)).astype(bf16)
            far_copy(k, at).start()

    def static(k):
        low, count = chunks[k]
        return pl.ds(low, count), low, count

    attend(0, *static(0))
    attend(1, *static(1))
    share(0, static(0)[0])
    full = rows // STEP

    def attend_full(index):
        attend(index + 1, block(index, STEP), index * STEP, STEP)

    if full > 1:
        attend_full(1)
    share(1, static(1)[0])

    def both(index, carry):
        attend_full(index + 1)
        share(index + 1, block(index, STEP))
        return carry

    lax.fori_loop(1, full - 1, both, 0)
    if full > 1:
        share(full, block(full - 1, STEP))
    with scope("keep"):
        own_sum[...] = mix(att_own, every, 0, 0) + mix(att_pair, every, 1, 0)

    for k, (low, count) in enumerate(chunks):
        at = pl.ds(low, count)
        with scope(f"far{k}"):
            far_copy(k, at).wait_recv()
        out[at, :] = (own_sum[at, :] + far_part[at, :].astype(f32)).astype(out.dtype)

    with scope("sent"):
        sent(tok, tok_sem.at[1])
        sent(wo.at[1], wo_sem.at[1])
        sent(att_own, a_send)
        crossed = sum(lengths[k] for k in crossing)
        straight = rows - crossed
        short = sum(lengths[k] for k in shortcut)

        def keys_sent(before):
            ahead = columns - 1 - before
            count = rows + ahead * (rows + crossed)
            count += straight * before
            if ahead == 0:
                count -= short
            if ahead == 1:
                count += short
            sent(weights.at[pl.ds(0, 2), pl.ds(0, count // 2), shared], kv_send)

        def direct_sent(shift, carry):
            sent(partial_keys, sends(0, shift))
            return carry

        def pair_sent(where, carry):
            sent(partial_keys, sends(1, where))
            return carry

        if early:
            at_place(keys_sent)
        else:
            partial_keys = far_send.at[:, shared]
            lax.fori_loop(1, later + 1, direct_sent, 0)
            lax.fori_loop(0, place + 1, pair_sent, 0)


def solution(mesh):
    n_ctx, n_head = mesh.shape["ctx"], mesh.shape["head"]

    def local(tokens, w_query, key_matrix, value_matrix, w_output):
        rows, depth = tokens.shape
        size = key_matrix.shape[1]
        heads = w_query.shape[1]
        group = heads // size
        columns = n_ctx // 2
        early = columns <= UNROLLED
        shares = SHORT_GROUPS if early else LONG_GROUPS
        unit = rows // sum(sum(share) for share in shares)
        sizes = [sum(share) * unit for share in shares]
        pieces = sum(len(share) for share in shares)
        groups = len(shares)
        chunks = rows // STEP + 1
        bf16, f32 = jnp.bfloat16, jnp.float32
        dma = pltpu.SemaphoreType.DMA
        vmem = pltpu.VMEM

        def found(length):
            if early:
                return vmem((group, rows, n_ctx * length), f32)
            return vmem((columns, group * STEP, 2 * length), f32)

        return pl.pallas_call(
            functools.partial(layer_kernel, n_ctx, n_head, shares, early),
            out_shape=vmem((rows, depth), bf16),
            in_specs=[pl.BlockSpec(memory_space=pltpu.HBM)] * 5,
            out_specs=pl.BlockSpec(memory_space=pltpu.VMEM),
            scratch_shapes=[
                vmem((n_head, depth, 2 * size + heads), bf16),
                vmem((2, 2, heads, depth), bf16),
                vmem((n_head, rows, depth), bf16),
                vmem((rows, 2 * size + heads), f32),
                vmem((group, rows, size), bf16),
                vmem((group, rows, LANES), f32),
                vmem((rows, heads), bf16),
                vmem((rows, heads), bf16),
                vmem((rows, depth), f32),
                vmem((rows, depth), bf16),
                vmem((rows, depth), bf16),
                *[vmem((n_ctx, length, 2 * size), bf16) for length in sizes],
                *[found(length) for length in sizes],
                dma((n_head,)),
                dma((3,)),
                dma((3,)),
                dma((pieces,)),
                dma((pieces,)),
                dma if early else dma((2, columns)),
                dma((columns - 1, pieces)),
                dma((groups,)) if early else dma((columns, groups)),
                dma,
                dma((chunks,)),
                dma((chunks,)),
                pltpu.SemaphoreType.REGULAR,
            ],
            compiler_params=pltpu.CompilerParams(
                collective_id=0,
                has_side_effects=True,
                vmem_limit_bytes=63 * 1024 * 1024,
            ),
        )(tokens, w_query, key_matrix, value_matrix, w_output)

    return jax.shard_map(
        local,
        mesh=mesh,
        in_specs=(
            P("ctx", "head"),
            P(None, "head"),
            P(None, "head"),
            P(None, "head"),
            P("head", None),
        ),
        out_specs=P("ctx", "head"),
        check_vma=False,
    )
```

```python
import functools
import math

import jax
import jax.numpy as jnp
from jax import lax
from jax.experimental import pallas as pl
from jax.experimental.pallas import tpu as pltpu
from jax.sharding import PartitionSpec as P

MESH = pl.DeviceIdType.MESH
SHORT_GROUPS = ((1, 1, 1, 1), (1, 1), (1, 1))
LONG_GROUPS = ((2,), (2,), (2,), (2,))
CROSSING = (7,)
FLYING = 4
LAG = 2
SHORTCUT = (0, 1, 2, 3, 4, 5, 6)
EARLY_SLOTS = 2
STEP = 64
LANES = 128
UNROLLED = 4
NEG_LARGE = -1e30

scope = jax.named_scope


def layer_kernel(n_ctx, n_head, shares, early, *refs):
    groups = len(shares)
    tokens, wq_hbm, wk_hbm, wv_hbm, wo_hbm, out = refs[:6]
    weights, wo, tok, partial, query, top_ref, att_own, att_pair = refs[6:14]
    own_sum, far_send, far_part = refs[14:17]
    kv = refs[17 : 17 + groups]
    scores = refs[17 + groups : 17 + 2 * groups]
    (
        w_sem,
        wo_sem,
        tok_sem,
        across_recv,
        diag_recv,
        kv_send,
        same_recv,
        other_recv,
        a_send,
        a_recv,
        r_recv,
        ready,
    ) = refs[17 + 2 * groups :]
    rows, depth = tokens.shape
    size = wk_hbm.shape[1]
    heads = wq_hbm.shape[1]
    group = heads // size
    c = lax.axis_index("ctx")
    h = lax.axis_index("head")
    place, side = c // 2, c % 2
    core = h % 2
    pair = h + 1 - 2 * core
    across = (h + 2) % n_head
    diag = across + 1 - 2 * core
    ctx_pair = c + 1 - 2 * side
    columns = n_ctx // 2
    later = columns - 1 - place
    at_end = later == 0
    f32, bf16 = jnp.float32, jnp.bfloat16
    every = slice(None)

    unit = rows // sum(sum(share) for share in shares)
    lengths, starts, owners, offsets, first_row = [], [], [], [], []
    row = 0
    for g, share in enumerate(shares):
        first_row.append(row)
        for count in share:
            owners.append(g)
            starts.append(row)
            offsets.append(row - first_row[g])
            lengths.append(count * unit)
            row += count * unit
    pieces = len(lengths)
    sizes = [sum(share) * unit for share in shares]
    last = pieces - 1
    crossing = CROSSING if early else ()
    shortcut = SHORTCUT if early else ()

    def remote(src, dst, send, recv, target):
        return pltpu.make_async_remote_copy(
            src_ref=src,
            dst_ref=dst,
            send_sem=send,
            recv_sem=recv,
            device_id=target,
            device_id_type=MESH,
        )

    def sent(ref, sem):
        remote(ref, ref, sem, sem, {"head": pair}).wait_send()

    def came(ref, sem):
        remote(ref, ref, sem, sem, {"head": pair}).wait_recv()

    def at_place(call):
        for before in range(columns):
            pl.when(place == before)(functools.partial(call, before))

    def block(index, count):
        return pl.ds(pl.multiple_of(index * count, count), count)

    def piece(k):
        return pl.ds(starts[k], lengths[k])

    own_load = pltpu.make_async_copy(tokens, tok.at[0], tok_sem.at[0])
    own_load.start()
    barrier = pltpu.get_barrier_semaphore()

    def greet(target):
        pl.semaphore_signal(barrier, inc=1, device_id=target, device_id_type=MESH)

    per_place = 2 if early else 1

    def greet_later(shift, carry):
        greet({"ctx": c + 2 * shift})
        if early:
            greet({"ctx": ctx_pair + 2 * shift})
        return carry

    def answer(where, carry):
        for which in (side, 1 - side)[:per_place]:
            pl.semaphore_signal(
                ready, inc=1, device_id={"ctx": 2 * where + which}, device_id_type=MESH
            )
        return carry

    greet({"head": pair})
    greet({"head": across})
    greet({"ctx": ctx_pair})
    lax.fori_loop(1, later + 1, greet_later, 0)
    with scope("own"):
        own_load.wait()
    def fetch(slot):
        at = block((h, pair, across, diag)[slot], depth)
        into = weights.at[slot]
        for src, low, width in (
            (wk_hbm, 0, size),
            (wv_hbm, size, size),
            (wq_hbm, 2 * size, heads),
        ):
            pltpu.make_async_copy(
                src.at[at], into.at[:, pl.ds(low, width)], w_sem.at[slot]
            ).start()

    def loaded(slot):
        pltpu.make_async_copy(weights.at[slot], weights.at[slot], w_sem.at[slot]).wait()

    for slot in range(EARLY_SLOTS):
        fetch(slot)
    with scope("barrier"):
        pl.semaphore_wait(barrier, 3 + per_place * place)

    def token_copy(k):
        return remote(
            tok.at[0, piece(k)],
            tok.at[2, piece(k)],
            tok_sem.at[1],
            across_recv.at[k],
            {"head": across},
        )

    def token_relay(k):
        return remote(
            tok.at[2, piece(k)],
            tok.at[3, piece(k)],
            tok_sem.at[1],
            diag_recv.at[k],
            {"head": pair},
        )

    for k in range(min(FLYING, pieces)):
        token_copy(k).start()
    pair_tokens = remote(tok.at[0], tok.at[1], tok_sem.at[1], tok_sem.at[2], {"head": pair})
    pair_tokens.start()
    lax.fori_loop(0, place, answer, 0)
    for slot in range(EARLY_SLOTS, n_head):
        fetch(slot)

    def fetch_output_weights(k):
        count = heads // pieces
        at = pl.ds(k * count, count)
        for slot, owner in enumerate((h, across)):
            pltpu.make_async_copy(
                wo_hbm.at[at, block(owner, depth)], wo.at[0, slot, at], wo_sem.at[0]
            ).start()
        for slot, owner in enumerate((pair, diag)):
            remote(
                wo_hbm.at[at, block(owner, depth)],
                wo.at[1, slot, at],
                wo_sem.at[1],
                wo_sem.at[2],
                {"head": pair},
            ).start()

    def kv_copy(which, k, send, recv, target):
        at = kv[owners[k]].at[which, pl.ds(offsets[k], lengths[k])]
        return remote(at, at, send, recv, {"ctx": target})

    def sends(kind, index):
        return kv_send if early else kv_send.at[kind, index]

    def others(where, g):
        return other_recv.at[g] if early else other_recv.at[where, g]

    def direct_copy(shift, k):
        return kv_copy(c, k, sends(0, shift), same_recv.at[place, k], c + 2 * shift)

    def cross_copy(shift, k):
        target = ctx_pair + 2 * shift
        return kv_copy(c, k, sends(0, shift), others(place, owners[k]), target)

    def pair_copy(where, k):
        recv = others(where, owners[k])
        return kv_copy(2 * where + side, k, sends(1, where), recv, ctx_pair)

    def same_arrived(where, k):
        at = kv[owners[k]].at[2 * where + side, pl.ds(offsets[k], lengths[k])]
        came(at, same_recv.at[where, k])

    def relayed(k):
        if k in crossing:
            return 0
        return jnp.where(at_end, place - 1, place) if k in shortcut else place

    def relay(k):
        def one(where, carry):
            same_arrived(where, k)
            pair_copy(where, k).start()
            return carry

        with scope(f"relay{k}"):
            lax.fori_loop(0, relayed(k), one, 0)

    def arrive(g):
        def other(where, carry):
            came(kv[g].at[2 * where + 1 - side], others(where, g))
            return carry

        def all_others(before):
            came(kv[g].at[pl.ds(0, before + 1)], other_recv.at[g])

        with scope(f"arrive{g}"):
            for k in range(pieces):
                if owners[k] == g:

                    def same(where, carry, k=k):
                        same_arrived(where, k)
                        return carry

                    lax.fori_loop(relayed(k), place, same, 0)
            if early:
                at_place(all_others)
            else:
                lax.fori_loop(0, place + 1, other, 0)

    shared, queries_at = pl.ds(0, 2 * size), pl.ds(2 * size, heads)

    def term(slot, at, wanted):
        return jnp.dot(
            tok[slot, at, :], weights[slot, :, wanted], preferred_element_type=f32
        )

    def begin():
        loaded(0)
        partial[...] = term(0, every, every)
        pair_tokens.wait_recv()
        loaded(1)
        partial[...] += term(1, every, every)
        loaded(2)
        loaded(3)

    def receive(k):
        with scope(f"across{k}"):
            token_copy(k).wait_recv()
        token_relay(k).start()
        if k + FLYING < pieces:
            token_copy(k + FLYING).start()
        fetch_output_weights(k)

    def finish_keys(k, found):
        with scope(f"diag{k}"):
            token_relay(k).wait_recv()
        found = found + term(3, piece(k), shared)
        kv[owners[k]][c, pl.ds(offsets[k], lengths[k]), :] = found.astype(bf16)

        def send(index, carry):
            shift = jnp.where(place == 0, index + 1, later - index)
            direct_copy(shift, k).start()
            if k in crossing:
                cross_copy(shift, k).start()
            return carry

        if k == 0:

            @pl.when(later > 0)
            def _():
                pl.semaphore_wait(ready, per_place * later)

        lax.fori_loop(0, later, send, 0)
        if k in shortcut:

            @pl.when(later == 1)
            def _():
                cross_copy(1, k).start()

        pair_copy(place, k).start()

    def finish_queries():
        found = partial[:, queries_at]
        for slot in (2, 3):
            found = found + term(slot, every, queries_at)
        for g in range(group):
            query[g] = found[:, g * size : (g + 1) * size].astype(bf16)

    with scope("begin"):
        begin()
    for k in range(pieces):
        if k == 0:
            receive(k)
        else:
            pl.when(core == 0)(functools.partial(receive, k))
        found = partial[piece(k), shared] + term(2, piece(k), shared)
        if k < last:
            pl.when(core == 1)(functools.partial(receive, k + 1))
        finish_keys(k, found)
        if k >= LAG:
            relay(k - LAG)
    with scope("queries"):
        finish_queries()
    waiting = list(range(max(pieces - LAG, 0), pieces))

    factor = (size ** (-0.5)) * math.log2(math.e)

    def fold(values, op):
        result = values[:, :LANES]
        for index in range(1, values.shape[1] // LANES):
            result = op(result, values[:, index * LANES : (index + 1) * LANES])
        return result

    def queries_of(at, count):
        return query[:, at, :].reshape(group * count, size)

    def product(queries, keys):
        return lax.dot_general(
            queries, keys, (((1,), (1,)), ((), ())), preferred_element_type=f32
        )

    def mask(found, low, count, g):
        width = found.shape[1]
        column = lax.broadcasted_iota(jnp.int32, (count, width), 1)
        shift = sizes[g].bit_length() - 1
        at_key = (column >> shift) * rows + (column & (sizes[g] - 1)) + first_row[g]
        at_query = lax.broadcasted_iota(jnp.int32, (count, width), 0) + low
        allowed = at_key <= at_query + side * rows
        return jnp.where(jnp.concatenate([allowed] * group, axis=0), found, NEG_LARGE)

    def keys_of(g, where, places):
        return kv[g][pl.ds(2 * where, 2 * places), :, pl.ds(0, size)].reshape(-1, size)

    def values_of(g, where, places):
        return kv[g][pl.ds(2 * where, 2 * places), :, pl.ds(size, size)].reshape(-1, size)

    def score(at, low, count, g, before):
        found = product(queries_of(at, count), keys_of(g, 0, before + 1))
        split = 2 * before * sizes[g]
        tail = mask(found[:, split:], low, count, g)
        scores[g][:, at, pl.ds(split, 2 * sizes[g])] = tail.reshape(group, count, -1)
        top = fold(tail, jnp.maximum)
        if split:
            head = found[:, :split]
            scores[g][:, at, pl.ds(0, split)] = head.reshape(group, count, split)
            top = jnp.maximum(top, fold(head, jnp.maximum))
        return top

    def weigh(found, top, values, state):
        total, summed = state
        weighed = jnp.exp2((found - top) * factor)
        summed = summed + jnp.dot(weighed.astype(bf16), values, preferred_element_type=f32)
        return total + fold(weighed, jnp.add), summed

    def close(at, count, state):
        total, summed = state
        total = jnp.sum(total, axis=-1, keepdims=True)
        mixed = (summed / total).astype(bf16)
        for g in range(group):
            att_own[at, pl.ds(g * size, size)] = mixed[g * count : (g + 1) * count]

    def nothing(count):
        return tuple(jnp.zeros((group * count, width), f32) for width in (LANES, size))

    def attention(at, low, count, before):
        top = top_ref[:, at, :].reshape(group * count, LANES)
        top = jnp.maximum(top, score(at, low, count, groups - 1, before))
        top = jnp.max(top, axis=-1, keepdims=True)
        state = nothing(count)
        for g in range(groups):
            width = 2 * (before + 1) * sizes[g]
            found = scores[g][:, at, pl.ds(0, width)].reshape(group * count, width)
            state = weigh(found, top, values_of(g, 0, before + 1), state)
        close(at, count, state)

    def attention_at_length(at, low, count):
        queries = queries_of(at, count)
        here = pl.ds(0, group * count)
        top = jnp.full((group * count, LANES), NEG_LARGE, f32)
        for g in range(groups):

            def first_pass(where, top, g=g):
                found = product(queries, keys_of(g, where, 1))
                scores[g][where, here] = found
                return jnp.maximum(top, fold(found, jnp.maximum))

            found = mask(product(queries, keys_of(g, place, 1)), low, count, g)
            scores[g][place, here] = found
            top = jnp.maximum(top, fold(found, jnp.maximum))
            top = lax.fori_loop(0, place, first_pass, top)
        top = jnp.max(top, axis=-1, keepdims=True)
        state = nothing(count)
        for g in range(groups):

            def second_pass(where, state, g=g):
                return weigh(scores[g][where, here], top, values_of(g, where, 1), state)

            state = lax.fori_loop(0, place + 1, second_pass, state)
        close(at, count, state)

    def prepare(g, begin, end):
        count = min(2 * STEP, rows)

        def run(before):
            def one(index, carry):
                at = block(index, count)
                top = score(at, index * count, count, g, before)
                top = top.reshape(group, count, LANES)
                if g > 0:
                    top = jnp.maximum(top, top_ref[:, at, :])
                top_ref[:, at, :] = top
                return carry

            lax.fori_loop(begin, end or rows // count, one, 0)

        with scope(f"prepare{g}"):
            at_place(run)

    for k in waiting:
        relay(k)
    if early:
        arrive(0)
        prepare(0, 0, None)
        for g in range(1, groups - 1):
            arrive(g)
            prepare(g, 0, 1 if g == groups - 2 else None)
        arrive(groups - 1)
    else:
        for g in range(groups):
            arrive(g)

    with scope("wo"):
        pltpu.make_async_copy(wo.at[0], wo.at[0], wo_sem.at[0]).wait()
        came(wo.at[1], wo_sem.at[2])

    chunks = [(0, STEP // 2), (STEP // 2, STEP // 2)]
    chunks += [(low, STEP) for low in range(STEP, rows, STEP)]

    def att_copy(k, at):
        return remote(
            att_own.at[at], att_pair.at[at], a_send, a_recv.at[k], {"head": pair}
        )

    def far_copy(k, at):
        return remote(
            far_send.at[at],
            far_part.at[at],
            tok_sem.at[1],
            r_recv.at[k],
            {"head": across},
        )

    def attend(k, at, low, count):
        with scope("attention"):
            if early:
                at_place(functools.partial(attention, at, low, count))
            else:
                attention_at_length(at, low, count)
        att_copy(k, at).start()

    def mix(ref, at, source, slot):
        return jnp.dot(ref[at, :], wo[source, slot], preferred_element_type=f32)

    def share(k, at):
        own = mix(att_own, at, 0, 1)
        with scope("exchange"):
            att_copy(k, at).wait_recv()
        with scope("mix"):
            far_send[at, :] = (own + mix(att_pair, at, 1, 1)).astype(bf16)
            far_copy(k, at).start()

    def static(k):
        low, count = chunks[k]
        return pl.ds(low, count), low, count

    attend(0, *static(0))
    attend(1, *static(1))
    share(0, static(0)[0])
    full = rows // STEP

    def attend_full(index):
        attend(index + 1, block(index, STEP), index * STEP, STEP)

    if full > 1:
        attend_full(1)
    share(1, static(1)[0])

    def both(index, carry):
        attend_full(index + 1)
        share(index + 1, block(index, STEP))
        return carry

    if full > 1:
        share(2, block(1, STEP))
    if early:
        prepare(groups - 2, 1, None)
    if full > 2:
        attend_full(2)
    lax.fori_loop(2, full - 1, both, 0)
    if full > 2:
        share(full, block(full - 1, STEP))
    with scope("keep"):
        own_sum[...] = mix(att_own, every, 0, 0) + mix(att_pair, every, 1, 0)

    for k, (low, count) in enumerate(chunks):
        at = pl.ds(low, count)
        with scope(f"far{k}"):
            far_copy(k, at).wait_recv()
        out[at, :] = (own_sum[at, :] + far_part[at, :].astype(f32)).astype(out.dtype)

    with scope("sent"):
        sent(tok, tok_sem.at[1])
        sent(wo.at[1], wo_sem.at[1])
        sent(att_own, a_send)
        crossed = sum(lengths[k] for k in crossing)
        straight = rows - crossed
        short = sum(lengths[k] for k in shortcut)

        def keys_sent(before):
            ahead = columns - 1 - before
            count = rows + ahead * (rows + crossed)
            count += straight * before
            if ahead == 0:
                count -= short
            if ahead == 1:
                count += short
            sent(weights.at[pl.ds(0, 2), pl.ds(0, count // 2), shared], kv_send)

        def direct_sent(shift, carry):
            sent(partial_keys, sends(0, shift))
            return carry

        def pair_sent(where, carry):
            sent(partial_keys, sends(1, where))
            return carry

        if early:
            at_place(keys_sent)
        else:
            partial_keys = far_send.at[:, shared]
            lax.fori_loop(1, later + 1, direct_sent, 0)
            lax.fori_loop(0, place + 1, pair_sent, 0)


def solution(mesh):
    n_ctx, n_head = mesh.shape["ctx"], mesh.shape["head"]

    def local(tokens, w_query, key_matrix, value_matrix, w_output):
        rows, depth = tokens.shape
        size = key_matrix.shape[1]
        heads = w_query.shape[1]
        group = heads // size
        columns = n_ctx // 2
        early = columns <= UNROLLED
        shares = SHORT_GROUPS if early else LONG_GROUPS
        unit = rows // sum(sum(share) for share in shares)
        sizes = [sum(share) * unit for share in shares]
        pieces = sum(len(share) for share in shares)
        groups = len(shares)
        chunks = rows // STEP + 1
        bf16, f32 = jnp.bfloat16, jnp.float32
        dma = pltpu.SemaphoreType.DMA
        vmem = pltpu.VMEM

        def found(length):
            if early:
                return vmem((group, rows, n_ctx * length), f32)
            return vmem((columns, group * STEP, 2 * length), f32)

        return pl.pallas_call(
            functools.partial(layer_kernel, n_ctx, n_head, shares, early),
            out_shape=vmem((rows, depth), bf16),
            in_specs=[pl.BlockSpec(memory_space=pltpu.HBM)] * 5,
            out_specs=pl.BlockSpec(memory_space=pltpu.VMEM),
            scratch_shapes=[
                vmem((n_head, depth, 2 * size + heads), bf16),
                vmem((2, 2, heads, depth), bf16),
                vmem((n_head, rows, depth), bf16),
                vmem((rows, 2 * size + heads), f32),
                vmem((group, rows, size), bf16),
                vmem((group, rows, LANES), f32),
                vmem((rows, heads), bf16),
                vmem((rows, heads), bf16),
                vmem((rows, depth), f32),
                vmem((rows, depth), bf16),
                vmem((rows, depth), bf16),
                *[vmem((n_ctx, length, 2 * size), bf16) for length in sizes],
                *[found(length) for length in sizes],
                dma((n_head,)),
                dma((3,)),
                dma((3,)),
                dma((pieces,)),
                dma((pieces,)),
                dma if early else dma((2, columns)),
                dma((columns - 1, pieces)),
                dma((groups,)) if early else dma((columns, groups)),
                dma,
                dma((chunks,)),
                dma((chunks,)),
                pltpu.SemaphoreType.REGULAR,
            ],
            compiler_params=pltpu.CompilerParams(
                collective_id=0,
                has_side_effects=True,
                vmem_limit_bytes=63 * 1024 * 1024,
            ),
        )(tokens, w_query, key_matrix, value_matrix, w_output)

    return jax.shard_map(
        local,
        mesh=mesh,
        in_specs=(
            P("ctx", "head"),
            P(None, "head"),
            P(None, "head"),
            P(None, "head"),
            P("head", None),
        ),
        out_specs=P("ctx", "head"),
        check_vma=False,
    )
```

```python
import functools
import math

import jax
import jax.numpy as jnp
from jax import lax
from jax.experimental import pallas as pl
from jax.experimental.pallas import tpu as pltpu
from jax.sharding import PartitionSpec as P

MESH = pl.DeviceIdType.MESH
SHORT_GROUPS = ((1, 1, 1, 1), (1, 1), (1, 1))
LONG_GROUPS = ((2,), (2,), (2,), (2,))
CROSSING = (7,)
FLYING = 4
LAG = 2
SHORTCUT = (0, 1, 2, 3, 4, 5, 6)
EARLY_SLOTS = 2
STEP = 64
LANES = 128
UNROLLED = 4
NEG_LARGE = -1e30

scope = jax.named_scope


def layer_kernel(n_ctx, n_head, shares, early, *refs):
    groups = len(shares)
    tokens, wq_hbm, wk_hbm, wv_hbm, wo_hbm, out = refs[:6]
    weights, wo, tok, partial, query, top_ref, att_own, att_pair = refs[6:14]
    own_sum, far_send, far_part = refs[14:17]
    kv = refs[17 : 17 + groups]
    scores = refs[17 + groups : 17 + 2 * groups]
    (
        w_sem,
        wo_sem,
        tok_sem,
        across_recv,
        diag_recv,
        kv_send,
        same_recv,
        other_recv,
        a_send,
        a_recv,
        r_recv,
        ready,
    ) = refs[17 + 2 * groups :]
    rows, depth = tokens.shape
    size = wk_hbm.shape[1]
    heads = wq_hbm.shape[1]
    group = heads // size
    c = lax.axis_index("ctx")
    h = lax.axis_index("head")
    place, side = c // 2, c % 2
    core = h % 2
    pair = h + 1 - 2 * core
    across = (h + 2) % n_head
    diag = across + 1 - 2 * core
    ctx_pair = c + 1 - 2 * side
    columns = n_ctx // 2
    later = columns - 1 - place
    at_end = later == 0
    f32, bf16 = jnp.float32, jnp.bfloat16
    every = slice(None)

    unit = rows // sum(sum(share) for share in shares)
    lengths, starts, owners, offsets, first_row = [], [], [], [], []
    row = 0
    for g, share in enumerate(shares):
        first_row.append(row)
        for count in share:
            owners.append(g)
            starts.append(row)
            offsets.append(row - first_row[g])
            lengths.append(count * unit)
            row += count * unit
    pieces = len(lengths)
    sizes = [sum(share) * unit for share in shares]
    last = pieces - 1
    crossing = CROSSING if early else ()
    shortcut = SHORTCUT if early else ()

    def remote(src, dst, send, recv, target):
        return pltpu.make_async_remote_copy(
            src_ref=src,
            dst_ref=dst,
            send_sem=send,
            recv_sem=recv,
            device_id=target,
            device_id_type=MESH,
        )

    def sent(ref, sem):
        remote(ref, ref, sem, sem, {"head": pair}).wait_send()

    def came(ref, sem):
        remote(ref, ref, sem, sem, {"head": pair}).wait_recv()

    def at_place(call):
        for before in range(columns):
            pl.when(place == before)(functools.partial(call, before))

    def block(index, count):
        return pl.ds(pl.multiple_of(index * count, count), count)

    def piece(k):
        return pl.ds(starts[k], lengths[k])

    own_load = pltpu.make_async_copy(tokens, tok.at[0], tok_sem.at[0])
    own_load.start()
    barrier = pltpu.get_barrier_semaphore()

    def greet(target):
        pl.semaphore_signal(barrier, inc=1, device_id=target, device_id_type=MESH)

    per_place = 2 if early else 1

    def greet_later(shift, carry):
        greet({"ctx": c + 2 * shift})
        if early:
            greet({"ctx": ctx_pair + 2 * shift})
        return carry

    def answer(where, carry):
        for which in (side, 1 - side)[:per_place]:
            pl.semaphore_signal(
                ready, inc=1, device_id={"ctx": 2 * where + which}, device_id_type=MESH
            )
        return carry

    greet({"head": pair})
    greet({"head": across})
    greet({"ctx": ctx_pair})
    lax.fori_loop(1, later + 1, greet_later, 0)
    with scope("own"):
        own_load.wait()
    def fetch(slot):
        at = block((h, pair, across, diag)[slot], depth)
        into = weights.at[slot]
        for src, low, width in (
            (wk_hbm, 0, size),
            (wv_hbm, size, size),
            (wq_hbm, 2 * size, heads),
        ):
            pltpu.make_async_copy(
                src.at[at], into.at[:, pl.ds(low, width)], w_sem.at[slot]
            ).start()

    def loaded(slot):
        pltpu.make_async_copy(weights.at[slot], weights.at[slot], w_sem.at[slot]).wait()

    for slot in range(EARLY_SLOTS):
        fetch(slot)
    with scope("barrier"):
        pl.semaphore_wait(barrier, 3 + per_place * place)

    def token_copy(k):
        return remote(
            tok.at[0, piece(k)],
            tok.at[2, piece(k)],
            tok_sem.at[1],
            across_recv.at[k],
            {"head": across},
        )

    def token_relay(k):
        return remote(
            tok.at[2, piece(k)],
            tok.at[3, piece(k)],
            tok_sem.at[1],
            diag_recv.at[k],
            {"head": pair},
        )

    for k in range(min(FLYING, pieces)):
        token_copy(k).start()
    pair_tokens = remote(tok.at[0], tok.at[1], tok_sem.at[1], tok_sem.at[2], {"head": pair})
    pair_tokens.start()
    lax.fori_loop(0, place, answer, 0)
    for slot in range(EARLY_SLOTS, n_head):
        fetch(slot)

    def fetch_output_weights(k):
        count = heads // pieces
        at = pl.ds(k * count, count)
        for slot, owner in enumerate((h, across)):
            pltpu.make_async_copy(
                wo_hbm.at[at, block(owner, depth)], wo.at[0, slot, at], wo_sem.at[0]
            ).start()
        for slot, owner in enumerate((pair, diag)):
            remote(
                wo_hbm.at[at, block(owner, depth)],
                wo.at[1, slot, at],
                wo_sem.at[1],
                wo_sem.at[2],
                {"head": pair},
            ).start()

    def kv_copy(which, k, send, recv, target):
        at = kv[owners[k]].at[which, pl.ds(offsets[k], lengths[k])]
        return remote(at, at, send, recv, {"ctx": target})

    def sends(kind, index):
        return kv_send if early else kv_send.at[kind, index]

    def others(where, g):
        return other_recv.at[g] if early else other_recv.at[where, g]

    def direct_copy(shift, k):
        return kv_copy(c, k, sends(0, shift), same_recv.at[place, k], c + 2 * shift)

    def cross_copy(shift, k):
        target = ctx_pair + 2 * shift
        return kv_copy(c, k, sends(0, shift), others(place, owners[k]), target)

    def pair_copy(where, k):
        recv = others(where, owners[k])
        return kv_copy(2 * where + side, k, sends(1, where), recv, ctx_pair)

    def same_arrived(where, k):
        at = kv[owners[k]].at[2 * where + side, pl.ds(offsets[k], lengths[k])]
        came(at, same_recv.at[where, k])

    def relayed(k):
        if k in crossing:
            return 0
        return jnp.where(at_end, place - 1, place) if k in shortcut else place

    def relay(k):
        def one(where, carry):
            same_arrived(where, k)
            pair_copy(where, k).start()
            return carry

        with scope(f"relay{k}"):
            lax.fori_loop(0, relayed(k), one, 0)

    def arrive(g):
        def other(where, carry):
            came(kv[g].at[2 * where + 1 - side], others(where, g))
            return carry

        def all_others(before):
            came(kv[g].at[pl.ds(0, before + 1)], other_recv.at[g])

        with scope(f"arrive{g}"):
            for k in range(pieces):
                if owners[k] == g:

                    def same(where, carry, k=k):
                        same_arrived(where, k)
                        return carry

                    lax.fori_loop(relayed(k), place, same, 0)
            if early:
                at_place(all_others)
            else:
                lax.fori_loop(0, place + 1, other, 0)

    shared, queries_at = pl.ds(0, 2 * size), pl.ds(2 * size, heads)

    def term(slot, at, wanted):
        return jnp.dot(
            tok[slot, at, :], weights[slot, :, wanted], preferred_element_type=f32
        )

    def begin():
        loaded(0)
        partial[...] = term(0, every, every)
        pair_tokens.wait_recv()
        loaded(1)
        partial[...] += term(1, every, every)
        loaded(2)
        loaded(3)

    def receive(k):
        with scope(f"across{k}"):
            token_copy(k).wait_recv()
        token_relay(k).start()
        if k + FLYING < pieces:
            token_copy(k + FLYING).start()
        fetch_output_weights(k)

    def finish_keys(k, found):
        with scope(f"diag{k}"):
            token_relay(k).wait_recv()
        found = found + term(3, piece(k), shared)
        kv[owners[k]][c, pl.ds(offsets[k], lengths[k]), :] = found.astype(bf16)

        def send(index, carry):
            shift = index + 1
            direct_copy(shift, k).start()
            if k in crossing:
                cross_copy(shift, k).start()
            return carry

        if k == 0:

            @pl.when(later > 0)
            def _():
                pl.semaphore_wait(ready, per_place * later)

        lax.fori_loop(0, later, send, 0)
        if k in shortcut:

            @pl.when(later == 1)
            def _():
                cross_copy(1, k).start()

        pair_copy(place, k).start()

    def finish_queries():
        found = partial[:, queries_at]
        for slot in (2, 3):
            found = found + term(slot, every, queries_at)
        for g in range(group):
            query[g] = found[:, g * size : (g + 1) * size].astype(bf16)

    with scope("begin"):
        begin()
    for k in range(pieces):
        if k == 0:
            receive(k)
        else:
            pl.when(core == 0)(functools.partial(receive, k))
        found = partial[piece(k), shared] + term(2, piece(k), shared)
        if k < last:
            pl.when(core == 1)(functools.partial(receive, k + 1))
        finish_keys(k, found)
        if k >= LAG:
            relay(k - LAG)
    with scope("queries"):
        finish_queries()
    waiting = list(range(max(pieces - LAG, 0), pieces))

    factor = (size ** (-0.5)) * math.log2(math.e)

    def fold(values, op):
        result = values[:, :LANES]
        for index in range(1, values.shape[1] // LANES):
            result = op(result, values[:, index * LANES : (index + 1) * LANES])
        return result

    def queries_of(at, count):
        return query[:, at, :].reshape(group * count, size)

    def product(queries, keys):
        return lax.dot_general(
            queries, keys, (((1,), (1,)), ((), ())), preferred_element_type=f32
        )

    def mask(found, low, count, g):
        width = found.shape[1]
        column = lax.broadcasted_iota(jnp.int32, (count, width), 1)
        shift = sizes[g].bit_length() - 1
        at_key = (column >> shift) * rows + (column & (sizes[g] - 1)) + first_row[g]
        at_query = lax.broadcasted_iota(jnp.int32, (count, width), 0) + low
        allowed = at_key <= at_query + side * rows
        return jnp.where(jnp.concatenate([allowed] * group, axis=0), found, NEG_LARGE)

    def keys_of(g, where, places):
        return kv[g][pl.ds(2 * where, 2 * places), :, pl.ds(0, size)].reshape(-1, size)

    def values_of(g, where, places):
        return kv[g][pl.ds(2 * where, 2 * places), :, pl.ds(size, size)].reshape(-1, size)

    def score(at, low, count, g, before):
        found = product(queries_of(at, count), keys_of(g, 0, before + 1))
        split = 2 * before * sizes[g]
        tail = mask(found[:, split:], low, count, g)
        scores[g][:, at, pl.ds(split, 2 * sizes[g])] = tail.reshape(group, count, -1)
        top = fold(tail, jnp.maximum)
        if split:
            head = found[:, :split]
            scores[g][:, at, pl.ds(0, split)] = head.reshape(group, count, split)
            top = jnp.maximum(top, fold(head, jnp.maximum))
        return top

    def weigh(found, top, values, state):
        total, summed = state
        weighed = jnp.exp2((found - top) * factor)
        summed = summed + jnp.dot(weighed.astype(bf16), values, preferred_element_type=f32)
        return total + fold(weighed, jnp.add), summed

    def close(at, count, state):
        total, summed = state
        total = jnp.sum(total, axis=-1, keepdims=True)
        mixed = (summed / total).astype(bf16)
        for g in range(group):
            att_own[at, pl.ds(g * size, size)] = mixed[g * count : (g + 1) * count]

    def nothing(count):
        return tuple(jnp.zeros((group * count, width), f32) for width in (LANES, size))

    def attention(at, low, count, before):
        top = top_ref[:, at, :].reshape(group * count, LANES)
        top = jnp.maximum(top, score(at, low, count, groups - 1, before))
        top = jnp.max(top, axis=-1, keepdims=True)
        state = nothing(count)
        for g in range(groups):
            width = 2 * (before + 1) * sizes[g]
            found = scores[g][:, at, pl.ds(0, width)].reshape(group * count, width)
            state = weigh(found, top, values_of(g, 0, before + 1), state)
        close(at, count, state)

    def attention_at_length(at, low, count):
        queries = queries_of(at, count)
        here = pl.ds(0, group * count)
        top = jnp.full((group * count, LANES), NEG_LARGE, f32)
        for g in range(groups):

            def first_pass(where, top, g=g):
                found = product(queries, keys_of(g, where, 1))
                scores[g][where, here] = found
                return jnp.maximum(top, fold(found, jnp.maximum))

            found = mask(product(queries, keys_of(g, place, 1)), low, count, g)
            scores[g][place, here] = found
            top = jnp.maximum(top, fold(found, jnp.maximum))
            top = lax.fori_loop(0, place, first_pass, top)
        top = jnp.max(top, axis=-1, keepdims=True)
        state = nothing(count)
        for g in range(groups):

            def second_pass(where, state, g=g):
                return weigh(scores[g][where, here], top, values_of(g, where, 1), state)

            state = lax.fori_loop(0, place + 1, second_pass, state)
        close(at, count, state)

    def prepare(g, begin, end):
        count = min(2 * STEP, rows)

        def run(before):
            def one(index, carry):
                at = block(index, count)
                top = score(at, index * count, count, g, before)
                top = top.reshape(group, count, LANES)
                if g > 0:
                    top = jnp.maximum(top, top_ref[:, at, :])
                top_ref[:, at, :] = top
                return carry

            lax.fori_loop(begin, end or rows // count, one, 0)

        with scope(f"prepare{g}"):
            at_place(run)

    for k in waiting:
        relay(k)
    if early:
        arrive(0)
        prepare(0, 0, None)
        for g in range(1, groups - 1):
            arrive(g)
            prepare(g, 0, 1 if g == groups - 2 else None)
        arrive(groups - 1)
    else:
        for g in range(groups):
            arrive(g)

    with scope("wo"):
        pltpu.make_async_copy(wo.at[0], wo.at[0], wo_sem.at[0]).wait()
        came(wo.at[1], wo_sem.at[2])

    chunks = [(0, STEP // 2), (STEP // 2, STEP // 2)]
    chunks += [(low, STEP) for low in range(STEP, rows, STEP)]

    def att_copy(k, at):
        return remote(
            att_own.at[at], att_pair.at[at], a_send, a_recv.at[k], {"head": pair}
        )

    def far_copy(k, at):
        return remote(
            far_send.at[at],
            far_part.at[at],
            tok_sem.at[1],
            r_recv.at[k],
            {"head": across},
        )

    def attend(k, at, low, count):
        with scope("attention"):
            if early:
                at_place(functools.partial(attention, at, low, count))
            else:
                attention_at_length(at, low, count)
        att_copy(k, at).start()

    def mix(ref, at, source, slot):
        return jnp.dot(ref[at, :], wo[source, slot], preferred_element_type=f32)

    def share(k, at):
        own = mix(att_own, at, 0, 1)
        with scope("exchange"):
            att_copy(k, at).wait_recv()
        with scope("mix"):
            far_send[at, :] = (own + mix(att_pair, at, 1, 1)).astype(bf16)
            far_copy(k, at).start()

    def static(k):
        low, count = chunks[k]
        return pl.ds(low, count), low, count

    attend(0, *static(0))
    attend(1, *static(1))
    share(0, static(0)[0])
    full = rows // STEP

    def attend_full(index):
        attend(index + 1, block(index, STEP), index * STEP, STEP)

    if full > 1:
        attend_full(1)
    share(1, static(1)[0])

    def both(index, carry):
        attend_full(index + 1)
        share(index + 1, block(index, STEP))
        return carry

    if full > 1:
        share(2, block(1, STEP))
    if early:
        prepare(groups - 2, 1, None)
    if full > 2:
        attend_full(2)
    lax.fori_loop(2, full - 1, both, 0)
    if full > 2:
        share(full, block(full - 1, STEP))
    with scope("keep"):
        own_sum[...] = mix(att_own, every, 0, 0) + mix(att_pair, every, 1, 0)

    for k, (low, count) in enumerate(chunks):
        at = pl.ds(low, count)
        with scope(f"far{k}"):
            far_copy(k, at).wait_recv()
        out[at, :] = (own_sum[at, :] + far_part[at, :].astype(f32)).astype(out.dtype)

    with scope("sent"):
        sent(tok, tok_sem.at[1])
        sent(wo.at[1], wo_sem.at[1])
        sent(att_own, a_send)
        crossed = sum(lengths[k] for k in crossing)
        straight = rows - crossed
        short = sum(lengths[k] for k in shortcut)

        def keys_sent(before):
            ahead = columns - 1 - before
            count = rows + ahead * (rows + crossed)
            count += straight * before
            if ahead == 0:
                count -= short
            if ahead == 1:
                count += short
            sent(weights.at[pl.ds(0, 2), pl.ds(0, count // 2), shared], kv_send)

        def direct_sent(shift, carry):
            sent(partial_keys, sends(0, shift))
            return carry

        def pair_sent(where, carry):
            sent(partial_keys, sends(1, where))
            return carry

        if early:
            at_place(keys_sent)
        else:
            partial_keys = far_send.at[:, shared]
            lax.fori_loop(1, later + 1, direct_sent, 0)
            lax.fori_loop(0, place + 1, pair_sent, 0)


def solution(mesh):
    n_ctx, n_head = mesh.shape["ctx"], mesh.shape["head"]

    def local(tokens, w_query, key_matrix, value_matrix, w_output):
        rows, depth = tokens.shape
        size = key_matrix.shape[1]
        heads = w_query.shape[1]
        group = heads // size
        columns = n_ctx // 2
        early = columns <= UNROLLED
        shares = SHORT_GROUPS if early else LONG_GROUPS
        unit = rows // sum(sum(share) for share in shares)
        sizes = [sum(share) * unit for share in shares]
        pieces = sum(len(share) for share in shares)
        groups = len(shares)
        chunks = rows // STEP + 1
        bf16, f32 = jnp.bfloat16, jnp.float32
        dma = pltpu.SemaphoreType.DMA
        vmem = pltpu.VMEM

        def found(length):
            if early:
                return vmem((group, rows, n_ctx * length), f32)
            return vmem((columns, group * STEP, 2 * length), f32)

        return pl.pallas_call(
            functools.partial(layer_kernel, n_ctx, n_head, shares, early),
            out_shape=vmem((rows, depth), bf16),
            in_specs=[pl.BlockSpec(memory_space=pltpu.HBM)] * 5,
            out_specs=pl.BlockSpec(memory_space=pltpu.VMEM),
            scratch_shapes=[
                vmem((n_head, depth, 2 * size + heads), bf16),
                vmem((2, 2, heads, depth), bf16),
                vmem((n_head, rows, depth), bf16),
                vmem((rows, 2 * size + heads), f32),
                vmem((group, rows, size), bf16),
                vmem((group, rows, LANES), f32),
                vmem((rows, heads), bf16),
                vmem((rows, heads), bf16),
                vmem((rows, depth), f32),
                vmem((rows, depth), bf16),
                vmem((rows, depth), bf16),
                *[vmem((n_ctx, length, 2 * size), bf16) for length in sizes],
                *[found(length) for length in sizes],
                dma((n_head,)),
                dma((3,)),
                dma((3,)),
                dma((pieces,)),
                dma((pieces,)),
                dma if early else dma((2, columns)),
                dma((columns - 1, pieces)),
                dma((groups,)) if early else dma((columns, groups)),
                dma,
                dma((chunks,)),
                dma((chunks,)),
                pltpu.SemaphoreType.REGULAR,
            ],
            compiler_params=pltpu.CompilerParams(
                collective_id=0,
                has_side_effects=True,
                vmem_limit_bytes=63 * 1024 * 1024,
            ),
        )(tokens, w_query, key_matrix, value_matrix, w_output)

    return jax.shard_map(
        local,
        mesh=mesh,
        in_specs=(
            P("ctx", "head"),
            P(None, "head"),
            P(None, "head"),
            P(None, "head"),
            P("head", None),
        ),
        out_specs=P("ctx", "head"),
        check_vma=False,
    )
```
